128 devices in a mesh: corr: 4 (over x), tile: 32 (over z, y, core).
Axes of the slice: x: 4, y: 4, z: 4, core: 2. Of those that a mesh axis runs over, the one named last changes fastest.
Arguments:
- visibilities: bfloat16 [8192, 8, 256], P(('corr', 'tile')), may hold values from -6 to 6
- coords: float32 [8192, 3, 256], P(('corr', 'tile')), may hold values from -12 to 12
- stations: int32 [8192, 2], P(('corr', 'tile')), may hold values from 0 to 511
- tile_ids: int32 [8192, 1], P(('corr', 'tile')), may hold values from 0 to 63; in each aligned block of 64 rows (0 to 63, 64 to 127, ...) at most 2 rows name the same one
- offsets: int32 [8192, 2], P(('corr', 'tile')), may hold values from 0 to 96
- screens: bfloat16 [512, 8, 1024], P('tile'), may hold values from -4 to 4
Outputs:
- grid_tiles: float32 [4, 64, 2, 128, 128], P('corr', 'tile')
The draws below stay inside these ranges and needn't reach their ends.
Inputs may be any that keep to these rules, and one draw needn't show every extreme that they name: `tile_ids`: within the rows of one device (aligned blocks of 64 rows) no uv-tile is named more than 2 times, and some uv-tile exactly 2 times.
All inputs are finite; a program needn't handle non-finite values.
Results may differ from the reference program's by a relative error of at most 0.0061.
Values may be sent and summed in bfloat16 or wider, within the bound.
A program may use at most 64 MiB of HBM per device.

```python
import math
import jax
import jax.numpy as jnp
import numpy as np
from jax import lax

NCORR = 4
SUB = 32
STATIONS = 512
NT = 64
TILE_SIDE = 128
SG_DEV = 64
NVIS = 256
PIX = 1024
SUBGRIDS = 8192
CAP = 2


def plant(result, stream_key, low, top_value):
    longest = result.shape.index(max(result.shape))
    spots = []
    for shift in (0, 1):
        where = [jax.random.randint(jax.random.fold_in(stream_key, axis), (), 0, length) for axis, length in enumerate(result.shape)]
        where[longest] = (where[longest] + shift) % result.shape[longest]
        spots.append(tuple(where))
    return result.at[spots[0]].set(low).at[spots[1]].set(top_value)


def level_of(rng, shape, cuts, smallest, top_value):
    factor_of = 1.0
    for axis_at, blocks in cuts:
        heights = jax.random.uniform(jax.random.fold_in(jax.random.fold_in(rng, 6), axis_at), (blocks,), jnp.float32, smallest / len(cuts), top_value / len(cuts))
        factor_of = factor_of * jnp.repeat(jnp.exp(heights), shape[axis_at] // blocks).reshape((-1,) + (1,) * (len(shape) - 1 - axis_at))
    return factor_of


def routed_block(stream_key, own, number, rows, amount, top, reach, slope):
    sequence = jax.random.permutation(stream_key, amount)
    crowded, common = load_shares(amount, rows * top, reach, slope, True), load_shares(amount, rows * top, reach, slope, False)
    places = jnp.arange(amount)

    def named(tallies, turn):
        used = int((tallies > 0).sum())
        fixed = max(1, used // 4)
        passed = fixed + (places - fixed + turn * (used - fixed)) % max(1, amount - fixed)
        return jnp.zeros((amount,), jnp.int32).at[sequence[jnp.where(places < fixed, places, passed)]].set(jnp.asarray(tallies, jnp.int32))

    tallies = jnp.where(number % 4 == 0, named(crowded, number // 4), named(common, number - number // 4 - 1))
    mixed = jax.random.permutation(jax.random.fold_in(own, 3), amount)
    source_of, taker = mixed[0:amount // 2 * 2:2], mixed[1:amount // 2 * 2:2]
    margin = jnp.minimum(tallies[source_of] - 1, reach - tallies[taker]) // 2
    margin = jnp.where((source_of == sequence[0]) | (taker == sequence[0]) | (tallies[taker] == 0), 0, jnp.maximum(margin, 0))
    passed = jax.random.randint(jax.random.fold_in(own, 4), (amount // 2,), 0, 1 << 20) % (margin + 1)
    tallies = tallies.at[source_of].add(-passed).at[taker].add(passed)
    labels = jnp.searchsorted(jnp.cumsum(tallies), jnp.arange(rows * top), side="right").astype(jnp.int32)
    table = labels.reshape(top, rows).T
    table = table[jax.random.permutation(jax.random.fold_in(own, 1), rows)]
    turn = jax.random.randint(jax.random.fold_in(own, 2), (rows, 1), 0, top)
    return jnp.take_along_axis(table, (jnp.arange(top)[None, :] + turn) % top, axis=1)


def load_shares(amount, total, most, lean, full):
    weights = [(1 << 20) // math.isqrt(rank ** lean) + 1 for rank in range(1, amount + 1)]
    largest = most if full else min(most, max(-(-total // amount), total * weights[0] // sum(weights)))
    least = 1 if total - largest >= amount - 1 else 0
    given, surplus = [largest] + [least] * (amount - 1), total - largest - least * (amount - 1)
    while surplus > 0:
        candidates = [i for i in range(1, amount) if given[i] < largest] or [i for i in range(1, amount) if given[i] < most]
        mass, budget = sum([weights[i] for i in candidates]), surplus
        for i in candidates:
            more = min(most - given[i], max(1, budget * weights[i] // mass), surplus)
            given[i] = given[i] + more
            surplus = surplus - more
    return np.array(given)


def centred(stream_key, dims, deviation, bound, shards=(), kind=jnp.bfloat16):
    level = level_of(stream_key, dims, shards, -0.22, 0.18) if shards else 1.0
    drawn = jax.random.normal(stream_key, dims, jnp.float32) * deviation * level
    return jnp.minimum(jnp.maximum(drawn, -bound), bound).astype(kind)


def setup_inputs(seed: int = 0) -> dict:
    arg_keys = jax.random.split(jax.random.key(seed), 7)
    visibilities = centred(arg_keys[0], (SUBGRIDS, 2 * NCORR, NVIS), 1.0, 6.0, ((0, 128),))
    coords = jnp.clip(jax.random.uniform(arg_keys[1], (SUBGRIDS, 3, NVIS), jnp.float32, -12.0, 12.0) * level_of(arg_keys[1], (SUBGRIDS, 3, NVIS), ((0, 128),), -0.4, 0.0), -12.0, 12.0)
    stations = plant(jax.random.randint(arg_keys[2], (SUBGRIDS, 2), 0, STATIONS), jax.random.fold_in(arg_keys[2], 1), 0, STATIONS - 1).astype(jnp.int32)
    tile_ids_keys = jax.random.split(jax.random.fold_in(arg_keys[3], 1), SUBGRIDS // SG_DEV)
    tile_ids_turns = jax.random.permutation(jax.random.fold_in(arg_keys[3], 3), SUBGRIDS // SG_DEV)
    tile_ids = jax.vmap(lambda own, number: routed_block(jax.random.fold_in(arg_keys[3], 2), own, number, SG_DEV, NT, 1, CAP, 2))(tile_ids_keys, tile_ids_turns).reshape((SUBGRIDS, 1))
    offsets = plant(jax.random.randint(arg_keys[4], (SUBGRIDS, 2), 0, TILE_SIDE - SUB + 1), jax.random.fold_in(arg_keys[4], 1), 0, TILE_SIDE - SUB).astype(jnp.int32)
    screens = centred(arg_keys[5], (STATIONS, 2 * NCORR, PIX), 0.7, 4.0, ((0, 32),))
    return dict(visibilities=visibilities, coords=coords, stations=stations, tile_ids=tile_ids, offsets=offsets, screens=screens)


def dft_table(scale):
    index = jnp.arange(SUB, dtype=jnp.int32) - SUB // 2
    product = (index[:, None] * index[None, :]) % SUB
    angle = (-2.0 * math.pi / SUB) * product.astype(jnp.float32)
    part_re = (jnp.cos(angle) * scale).astype(jnp.bfloat16)
    part_im = (jnp.sin(angle) * scale).astype(jnp.bfloat16)
    upper = jnp.stack([part_re, part_im], axis=1)
    lower = jnp.stack([-part_im, part_re], axis=1)
    return jnp.stack([upper, lower], axis=0)


def tables():
    pixel = jnp.arange(PIX, dtype=jnp.int32)
    row_index = pixel // SUB
    col_index = pixel % SUB
    centred_row = row_index - SUB // 2
    centred_col = col_index - SUB // 2
    coord_l = centred_row.astype(jnp.float32) / SUB
    coord_m = centred_col.astype(jnp.float32) / SUB
    coord_n = -0.5 * (coord_l * coord_l + coord_m * coord_m)
    half = SUB / 2.0
    row_pos = (row_index.astype(jnp.float32) - half + 0.5) / half
    col_pos = (col_index.astype(jnp.float32) - half + 0.5) / half
    taper = (1.0 - 0.8 * row_pos * row_pos) * (1.0 - 0.8 * col_pos * col_pos)
    return coord_l, coord_m, coord_n, taper, dft_table(1.0 / SUB), dft_table(1.0)


def sandwich(image_re, image_im, near, far):
    result_re = []
    result_im = []
    for row_out in range(2):
        for col_out in range(2):
            total_re = 0.0
            total_im = 0.0
            for inner in range(2):
                mid_re = 0.0
                mid_im = 0.0
                for first in range(2):
                    near_re = near[:, 2 * first + row_out]
                    near_im = near[:, 4 + 2 * first + row_out]
                    vis_re = image_re[:, 2 * first + inner]
                    vis_im = image_im[:, 2 * first + inner]
                    mid_re = mid_re + near_re * vis_re + near_im * vis_im
                    mid_im = mid_im + near_re * vis_im - near_im * vis_re
                far_re = far[:, 2 * inner + col_out]
                far_im = far[:, 4 + 2 * inner + col_out]
                total_re = total_re + mid_re * far_re - mid_im * far_im
                total_im = total_im + mid_re * far_im + mid_im * far_re
            result_re.append(total_re)
            result_im.append(total_im)
    return jnp.stack(result_re, axis=1), jnp.stack(result_im, axis=1)


def image_blocks(visibilities, coords, near, far, tabs):
    coord_l, coord_m, coord_n, taper, col_table, row_table = tabs
    phase = (2.0 * math.pi) * (coords[:, 0, :, None] * coord_l[None, None, :] + coords[:, 1, :, None] * coord_m[None, None, :] + coords[:, 2, :, None] * coord_n[None, None, :])
    cosines = jnp.cos(phase).astype(jnp.bfloat16)
    sines = jnp.sin(phase).astype(jnp.bfloat16)
    vis_wide = visibilities.astype(jnp.float32)
    with_cos = jnp.einsum("bfv,bvp->bfp", vis_wide, cosines.astype(jnp.float32), precision=lax.Precision.HIGHEST)
    with_sin = jnp.einsum("bfv,bvp->bfp", vis_wide, sines.astype(jnp.float32), precision=lax.Precision.HIGHEST)
    image_re = (with_cos[:, :4] - with_sin[:, 4:]) * (1.0 / NVIS)
    image_im = (with_cos[:, 4:] + with_sin[:, :4]) * (1.0 / NVIS)
    out_re, out_im = sandwich(image_re, image_im, near, far)
    stacked = jnp.stack([out_re, out_im], axis=2) * taper[None, None, None, :]
    return stacked.astype(jnp.bfloat16)


def reference(visibilities, coords, stations, tile_ids, offsets, screens):
    tabs = tables()
    col_table = tabs[4].astype(jnp.float32)
    row_table = tabs[5].astype(jnp.float32)
    count = visibilities.shape[0]
    block = 16

    def one_block(item):
        vis_part, coord_part, station_part = item
        near = jnp.take(screens, station_part[:, 0], axis=0).astype(jnp.float32)
        far = jnp.take(screens, station_part[:, 1], axis=0).astype(jnp.float32)
        images = image_blocks(vis_part, coord_part, near, far, tabs)
        square = images.astype(jnp.float32).reshape(block * NCORR, 2, SUB, SUB)
        half_block = jnp.einsum("nirc,icod->nord", square, col_table, precision=lax.Precision.HIGHEST).astype(jnp.bfloat16)
        uv_square = jnp.einsum("nord,orpe->npde", half_block.astype(jnp.float32), row_table, precision=lax.Precision.HIGHEST)
        return uv_square.astype(jnp.bfloat16).reshape(block, NCORR, 2, PIX)

    blocks = lax.map(one_block, (visibilities.reshape(count // block, block, 2 * NCORR, NVIS), coords.reshape(count // block, block, 3, NVIS), stations.reshape(count // block, block, 2)))
    blocks = blocks.reshape(count, NCORR, 2, SUB, SUB)

    def place(grid, item):
        uv_block, tile_one, offset_one = item
        start = (jnp.int32(0), tile_one.astype(jnp.int32), jnp.int32(0), offset_one[0].astype(jnp.int32), offset_one[1].astype(jnp.int32))
        current = lax.dynamic_slice(grid, start, (NCORR, 1, 2, SUB, SUB))
        grid = lax.dynamic_update_slice(grid, current + uv_block.astype(jnp.float32)[:, None], start)
        return grid, None

    grid = jnp.zeros((NCORR, NT, 2, TILE_SIDE, TILE_SIDE), jnp.float32)
    grid, _ = lax.scan(place, grid, (blocks, tile_ids[:, 0], offsets))
    return grid
```

```python
import functools
import math

import jax
import jax.numpy as jnp
import numpy as np
from jax import lax
from jax.experimental import pallas as pl
from jax.experimental.pallas import tpu as pltpu
from jax.sharding import PartitionSpec as P

SUB = 32
NT = 64
TILE_SIDE = 128
NVIS = 256
PIX = 1024
NCORR = 4
CAP = 2
NJ = 8
LANES = 128
SIN_POLY = (3.141592579805584, -5.167706866167941, 2.550031193519298, -0.5980441939119835, 0.07721838615698538)
COS_POLY = (0.9999999532476082, -4.934792830619647, 4.058411352862557, -1.3318765680805114, 0.2196896110968953)
ROOT_HALF = math.sqrt(0.5)
VMEM_LIMIT = 60 * 1024 * 1024


def uv_tables():
    rr = np.arange(4)[:, None, None, None]
    c = np.arange(SUB)[None, :, None, None]
    a4 = np.arange(4)[None, None, :, None]
    d = np.arange(SUB)[None, None, None, :]
    half = SUB // 2
    tables = []
    for a8 in range(NJ):
        turns = (rr * (a8 + 8 * a4 - half) + (c - half) * (d - half)) % SUB
        angle = (-2.0 * np.pi / SUB) * turns.reshape(LANES, LANES)
        re, im = np.cos(angle) / SUB, np.sin(angle) / SUB
        tables.append(np.block([[re, im], [-im, re]]))
    return jnp.asarray(np.stack(tables), jnp.bfloat16)


def taper_table():
    pos = (np.arange(SUB) - SUB // 2 + 0.5) / (SUB // 2)
    edge = 1.0 - 0.8 * pos * pos
    return jnp.asarray((edge[:, None] * edge[None, :] / NVIS).reshape(NJ, LANES), jnp.float32)


def poly(square, coefficients):
    total = jnp.full_like(square, coefficients[-1])
    for coefficient in coefficients[-2::-1]:
        total = total * square + coefficient
    return total


def cos_sin_turns(turns):
    rest = turns - jnp.round(turns)
    square = rest * rest
    sine = rest * poly(square, SIN_POLY)
    cosine = poly(square, COS_POLY)
    twice = sine + sine
    return 1.0 - twice * sine, twice * cosine


def direction_tables():
    row = lax.broadcasted_iota(jnp.int32, (2 * SUB, NVIS), 0)
    r = (row % NJ) * 4 + row // NJ
    place = jnp.where(row < SUB, r, row - SUB)
    first = (place - SUB // 2).astype(jnp.float32) * (1.0 / SUB)
    return first, -0.5 * first * first


def image_of(coords, vis, first, second):
    u, v, w = coords[0:1], coords[1:2], coords[2:3]
    linear = jnp.concatenate([u * first[:SUB], v * first[SUB:]], axis=0)
    cosine, sine = cos_sin_turns(linear + w * second)
    row_re, row_im = cosine[:SUB], sine[:SUB]
    col_re, col_im = cosine[SUB:], sine[SUB:]
    vis = vis.astype(jnp.float32)
    lhs = []
    for rr in range(4):
        a_re, a_im = row_re[rr * NJ:(rr + 1) * NJ], row_im[rr * NJ:(rr + 1) * NJ]
        part_re, part_im = [], []
        for e in range(NCORR):
            v_re, v_im = vis[e:e + 1], vis[NCORR + e:NCORR + e + 1]
            part_re.append(v_re * a_re - v_im * a_im)
            part_im.append(v_re * a_im + v_im * a_re)
        lhs.append(jnp.concatenate([jnp.concatenate(part_re, axis=0), jnp.concatenate(part_im, axis=0)], axis=1))
    lhs = jnp.concatenate(lhs, axis=0).astype(jnp.bfloat16)
    upper = jnp.concatenate([col_re, -col_im], axis=1)
    lower = jnp.concatenate([col_im, col_re], axis=1)
    rhs = jnp.concatenate([upper, lower, upper, lower], axis=0).astype(jnp.bfloat16)
    out = lax.dot_general(lhs, rhs, (((1,), (1,)), ((), ())), preferred_element_type=jnp.float32)
    parts = [out[rr * SUB:(rr + 1) * SUB] for rr in range(4)]
    turned = [pltpu.roll(part, SUB, 1) for part in parts]
    lane = lax.broadcasted_iota(jnp.int32, (SUB, LANES), 1)

    def join(a, b, c, d):
        return jnp.where(lane < SUB, a, jnp.where(lane < 2 * SUB, b, jnp.where(lane < 3 * SUB, c, d)))

    image_re = join(parts[0], turned[1], parts[2], turned[3])
    image_im = join(turned[0], parts[1], turned[2], parts[3])
    return image_re, image_im


def images_kernel(vis_ref, coords_ref, out_ref):
    first, second = direction_tables()

    def step(s, carry):
        image_re, image_im = image_of(coords_ref[s], vis_ref[s], first, second)
        out_ref[s, 0:SUB] = image_re
        out_ref[s, SUB:2 * SUB] = image_im
        return carry

    lax.fori_loop(0, vis_ref.shape[0], step, 0, unroll=2)


def images(visibilities, coords):
    count = visibilities.shape[0]
    vmem = pl.BlockSpec(memory_space=pltpu.VMEM)
    return pl.pallas_call(
        images_kernel,
        out_shape=jax.ShapeDtypeStruct((count, 2 * SUB, LANES), jnp.float32),
        in_specs=[vmem, vmem],
        out_specs=vmem,
        compiler_params=pltpu.CompilerParams(vmem_limit_bytes=VMEM_LIMIT),
        cost_estimate=pl.CostEstimate(flops=count * 2 * 128 * 512 * 128, bytes_accessed=4 << 20, transcendentals=0),
        name="images",
    )(visibilities, coords)


def sandwich_of(image, near, far):
    def row(array, index):
        return array[index * NJ:(index + 1) * NJ]

    mid_re, mid_im = {}, {}
    for out_row in range(2):
        for inner in range(2):
            total_re = total_im = None
            for first in range(2):
                n_re, n_im = row(near, 2 * first + out_row), row(near, 4 + 2 * first + out_row)
                v_re, v_im = row(image, 2 * first + inner), row(image, 4 + 2 * first + inner)
                re = n_re * v_re + n_im * v_im
                im = n_re * v_im - n_im * v_re
                total_re = re if total_re is None else total_re + re
                total_im = im if total_im is None else total_im + im
            mid_re[out_row, inner], mid_im[out_row, inner] = total_re, total_im
    out_re, out_im = [], []
    for out_row in range(2):
        for out_col in range(2):
            total_re = total_im = None
            for inner in range(2):
                m_re, m_im = mid_re[out_row, inner], mid_im[out_row, inner]
                f_re, f_im = row(far, 2 * inner + out_col), row(far, 4 + 2 * inner + out_col)
                re = m_re * f_re - m_im * f_im
                im = m_re * f_im + m_im * f_re
                total_re = re if total_re is None else total_re + re
                total_im = im if total_im is None else total_im + im
            out_re.append(total_re)
            out_im.append(total_im)
    return out_re, out_im


def fft8(re, im):
    def add(x, y):
        return x[0] + y[0], x[1] + y[1]

    def sub(x, y):
        return x[0] - y[0], x[1] - y[1]

    def turn(x):
        return x[1], -x[0]

    def fft4(x):
        even_add, even_sub = add(x[0], x[2]), sub(x[0], x[2])
        odd_add, odd_sub = add(x[1], x[3]), turn(sub(x[1], x[3]))
        return [add(even_add, odd_add), add(even_sub, odd_sub), sub(even_add, odd_add), sub(even_sub, odd_sub)]

    x = list(zip(re, im))
    even, odd = fft4(x[0::2]), fft4(x[1::2])
    odd = [
        odd[0],
        ((odd[1][0] + odd[1][1]) * ROOT_HALF, (odd[1][1] - odd[1][0]) * ROOT_HALF),
        turn(odd[2]),
        ((odd[3][1] - odd[3][0]) * ROOT_HALF, (-odd[3][0] - odd[3][1]) * ROOT_HALF),
    ]
    out = [add(even[k], odd[k]) for k in range(4)] + [sub(even[k], odd[k]) for k in range(4)]
    return [(-o[0], -o[1]) if k % 2 else o for k, o in enumerate(out)]


def blocks_kernel(count, stations, tile_ids, offsets, image_ref, taper_ref, table_ref, screens, send_ref, meta_ref,
                  near_far, x_re, x_im, y_ref, u_re, u_im, used, sems):
    def fetch(s, which):
        return pltpu.make_async_copy(screens.at[stations[s, which]], near_far.at[s, which], sems.at[s, which])

    def start(s, carry):
        fetch(s, 0).start()
        fetch(s, 1).start()
        return carry

    lax.fori_loop(0, count, start, 0)

    def clear(i, carry):
        used[i] = 0
        return carry

    lax.fori_loop(0, NT, clear, 0)

    def clear_meta(i, carry):
        meta_ref[i] = -1
        return carry

    lax.fori_loop(0, NT * CAP, clear_meta, 0)
    taper = taper_ref[...]

    def sandwich(s, carry):
        fetch(s, 0).wait()
        fetch(s, 1).wait()
        near = near_far[s, 0].astype(jnp.float32)
        far = near_far[s, 1].astype(jnp.float32)
        out_re, out_im = sandwich_of(image_ref[s], near, far)
        for e in range(NCORR):
            rows = pl.ds(pl.multiple_of(s * SUB + e * NJ, NJ), NJ)
            x_re[rows] = out_re[e] * taper
            x_im[rows] = out_im[e] * taper
        return carry

    lax.fori_loop(0, count, sandwich, 0, unroll=2)

    chunk = 16

    def transform(i, carry):
        base = i * (chunk * NJ)
        re = [x_re[pl.ds(base + j, chunk, stride=NJ)] for j in range(NJ)]
        im = [x_im[pl.ds(base + j, chunk, stride=NJ)] for j in range(NJ)]
        rows = pl.ds(pl.multiple_of(i * chunk, chunk), chunk)
        for a8, (y_re, y_im) in enumerate(fft8(re, im)):
            y_ref[a8, rows, 0:LANES] = y_re.astype(jnp.bfloat16)
            y_ref[a8, rows, LANES:2 * LANES] = y_im.astype(jnp.bfloat16)
        return carry

    lax.fori_loop(0, count * NCORR // chunk, transform, 0)

    for a8 in range(NJ):
        out = jnp.dot(y_ref[a8], table_ref[a8], preferred_element_type=jnp.float32)
        u_re[pl.ds(a8, count * NCORR, stride=NJ)] = out[:, 0:LANES]
        u_im[pl.ds(a8, count * NCORR, stride=NJ)] = out[:, LANES:2 * LANES]

    def pack(s, carry):
        tile = tile_ids[s]
        rank = used[tile]
        used[tile] = rank + 1
        slot = tile * CAP + rank
        meta_ref[slot] = offsets[s, 0] * TILE_SIDE + offsets[s, 1]
        target = pl.ds(pl.multiple_of(slot * 2 * NJ, 2 * NJ), 2 * NJ)
        for e in range(NCORR):
            rows = pl.ds(pl.multiple_of(s * SUB + e * NJ, NJ), NJ)
            send_ref[e, target] = jnp.concatenate([u_re[rows], u_im[rows]], axis=0).astype(jnp.bfloat16)
        return carry

    lax.fori_loop(0, count, pack, 0, unroll=2)


def blocks(image, screens, stations, tile_ids, offsets):
    count = image.shape[0]
    vmem = pl.BlockSpec(memory_space=pltpu.VMEM)
    smem = pl.BlockSpec(memory_space=pltpu.SMEM)
    slots = NT * CAP
    points = count * NCORR
    return pl.pallas_call(
        functools.partial(blocks_kernel, count),
        out_shape=(
            jax.ShapeDtypeStruct((NCORR, slots * 2 * NJ, LANES), jnp.bfloat16),
            jax.ShapeDtypeStruct((slots,), jnp.int32),
        ),
        in_specs=[smem, smem, smem, vmem, vmem, vmem, pl.BlockSpec(memory_space=pl.ANY)],
        out_specs=(vmem, smem),
        scratch_shapes=[
            pltpu.VMEM((count, 2, 2 * SUB, LANES), jnp.bfloat16),
            pltpu.VMEM((points * NJ, LANES), jnp.float32),
            pltpu.VMEM((points * NJ, LANES), jnp.float32),
            pltpu.VMEM((NJ, points, 2 * LANES), jnp.bfloat16),
            pltpu.VMEM((points * NJ, LANES), jnp.float32),
            pltpu.VMEM((points * NJ, LANES), jnp.float32),
            pltpu.SMEM((NT,), jnp.int32),
            pltpu.SemaphoreType.DMA((count, 2)),
        ],
        compiler_params=pltpu.CompilerParams(vmem_limit_bytes=VMEM_LIMIT),
        name="blocks",
    )(stations, tile_ids, offsets, image, taper_table(), uv_tables(), screens)


def gather_kernel(sources, per_owner, meta, recv_ref, out_ref, acc):
    acc[...] = jnp.zeros_like(acc)
    lane = lax.broadcasted_iota(jnp.int32, (NJ, LANES), 1)
    slots = per_owner * CAP

    def step(src, carry):
        for slot in range(slots):
            place = meta[src * slots + slot]
            valid = place >= 0
            row0 = jnp.where(valid, place // TILE_SIDE, 0)
            col0 = jnp.where(valid, place % TILE_SIDE, 0)
            begin = jnp.where(valid, row0, 2 * LANES)
            inside = (lane >= begin) & (lane < begin + SUB)
            block = recv_ref[src, slot * 2 * NJ:(slot + 1) * 2 * NJ].astype(jnp.float32)
            for part in range(2):
                data = block[part * NJ:(part + 1) * NJ]
                for a4 in range(4):
                    shift = jnp.where(row0 >= a4 * SUB, row0 - a4 * SUB, row0 - a4 * SUB + LANES)
                    moved = jnp.where(inside, pltpu.roll(data, shift, 1), 0.0)
                    rows = pl.ds(col0 + NJ * a4, NJ)
                    acc[slot, part, rows] = acc[slot, part, rows] + moved
        return carry

    lax.fori_loop(0, sources, step, 0)
    for tile in range(per_owner):
        for part in range(2):
            total = acc[tile * CAP, part]
            for rank in range(1, CAP):
                total = total + acc[tile * CAP + rank, part]
            out_ref[tile, part] = total.T


def gather_blocks(received, meta, per_owner):
    sources = received.shape[0]
    vmem = pl.BlockSpec(memory_space=pltpu.VMEM)
    return pl.pallas_call(
        functools.partial(gather_kernel, sources, per_owner),
        out_shape=jax.ShapeDtypeStruct((per_owner, 2, TILE_SIDE, TILE_SIDE), jnp.float32),
        in_specs=[pl.BlockSpec(memory_space=pltpu.SMEM), vmem],
        out_specs=vmem,
        scratch_shapes=[pltpu.VMEM((per_owner * CAP, 2, TILE_SIDE, TILE_SIDE), jnp.float32)],
        compiler_params=pltpu.CompilerParams(vmem_limit_bytes=VMEM_LIMIT),
        name="accumulate",
    )(meta, received)


def per_device(visibilities, coords, stations, tile_ids, offsets, screens):
    tile_size = lax.axis_size("tile")
    corr_size = lax.axis_size("corr")
    per_owner = NT // tile_size
    own = screens.reshape(screens.shape[0], 2 * SUB, LANES)
    all_screens = lax.all_gather(own, "tile", axis=0, tiled=True)
    image = images(visibilities, coords)
    sending, meta = blocks(image, all_screens, stations, tile_ids[:, 0], offsets)
    rows = per_owner * CAP * 2 * NJ
    received = lax.all_to_all(
        sending.reshape(NCORR * tile_size, rows, LANES), ("corr", "tile"), split_axis=0, concat_axis=0, tiled=True
    )
    meta = jnp.broadcast_to(meta.reshape(1, tile_size, per_owner * CAP), (corr_size, tile_size, per_owner * CAP))
    got_meta = lax.all_to_all(
        meta.reshape(corr_size * tile_size, per_owner * CAP), ("corr", "tile"), split_axis=0, concat_axis=0, tiled=True
    )
    return gather_blocks(received, got_meta.reshape(-1), per_owner)[None]


def solution(mesh):
    return jax.shard_map(
        per_device,
        mesh=mesh,
        in_specs=(
            P(("corr", "tile"), None, None),
            P(("corr", "tile"), None, None),
            P(("corr", "tile"), None),
            P(("corr", "tile"), None),
            P(("corr", "tile"), None),
            P("tile", None, None),
        ),
        out_specs=P("corr", "tile", None, None, None),
        check_vma=False,
    )
```

```python
import functools
import math

import jax
import jax.numpy as jnp
import numpy as np
from jax import lax
from jax.experimental import pallas as pl
from jax.experimental.pallas import tpu as pltpu
from jax.sharding import PartitionSpec as P

SUB = 32
NT = 64
TILE_SIDE = 128
NVIS = 256
PIX = 1024
NCORR = 4
CAP = 2
NJ = 8
LANES = 128
SIN_POLY = (3.141592579805584, -5.167706866167941, 2.550031193519298, -0.5980441939119835, 0.07721838615698538)
COS_POLY = (0.9999999532476082, -4.934792830619647, 4.058411352862557, -1.3318765680805114, 0.2196896110968953)
ROOT_HALF = math.sqrt(0.5)
VMEM_LIMIT = 60 * 1024 * 1024


def uv_tables():
    rr = np.arange(4)[:, None, None, None]
    c = np.arange(SUB)[None, :, None, None]
    a4 = np.arange(4)[None, None, :, None]
    d = np.arange(SUB)[None, None, None, :]
    half = SUB // 2
    tables = []
    for a8 in range(NJ):
        turns = (rr * (a8 + 8 * a4 - half) + (c - half) * (d - half)) % SUB
        angle = (-2.0 * np.pi / SUB) * turns.reshape(LANES, LANES)
        re, im = np.cos(angle) / SUB, np.sin(angle) / SUB
        tables.append(np.block([[re, im], [-im, re]]))
    return jnp.asarray(np.stack(tables), jnp.bfloat16)


def taper_table():
    pos = (np.arange(SUB) - SUB // 2 + 0.5) / (SUB // 2)
    edge = 1.0 - 0.8 * pos * pos
    return jnp.asarray((edge[:, None] * edge[None, :] / NVIS).reshape(NJ, LANES), jnp.float32)


def poly(square, coefficients):
    total = jnp.full_like(square, coefficients[-1])
    for coefficient in coefficients[-2::-1]:
        total = total * square + coefficient
    return total


def cos_sin_turns(turns):
    rest = turns - jnp.round(turns)
    square = rest * rest
    sine = rest * poly(square, SIN_POLY)
    cosine = poly(square, COS_POLY)
    twice = sine + sine
    return 1.0 - twice * sine, twice * cosine


def direction_tables():
    row = lax.broadcasted_iota(jnp.int32, (2 * SUB, NVIS), 0)
    r = (row % NJ) * 4 + row // NJ
    place = jnp.where(row < SUB, r, row - SUB)
    first = (place - SUB // 2).astype(jnp.float32) * (1.0 / SUB)
    return first, -0.5 * first * first


def image_of(coords, vis, first, second):
    u, v, w = coords[0:1], coords[1:2], coords[2:3]
    linear = jnp.concatenate([u * first[:SUB], v * first[SUB:]], axis=0)
    cosine, sine = cos_sin_turns(linear + w * second)
    row_re, row_im = cosine[:SUB], sine[:SUB]
    col_re, col_im = cosine[SUB:], sine[SUB:]
    vis = vis.astype(jnp.float32)
    lhs = []
    for rr in range(4):
        a_re, a_im = row_re[rr * NJ:(rr + 1) * NJ], row_im[rr * NJ:(rr + 1) * NJ]
        part_re, part_im = [], []
        for e in range(NCORR):
            v_re, v_im = vis[e:e + 1], vis[NCORR + e:NCORR + e + 1]
            part_re.append(v_re * a_re - v_im * a_im)
            part_im.append(v_re * a_im + v_im * a_re)
        lhs.append(jnp.concatenate([jnp.concatenate(part_re, axis=0), jnp.concatenate(part_im, axis=0)], axis=1))
    lhs = jnp.concatenate(lhs, axis=0).astype(jnp.bfloat16)
    upper = jnp.concatenate([col_re, -col_im], axis=1)
    lower = jnp.concatenate([col_im, col_re], axis=1)
    rhs = jnp.concatenate([upper, lower, upper, lower], axis=0).astype(jnp.bfloat16)
    out = lax.dot_general(lhs, rhs, (((1,), (1,)), ((), ())), preferred_element_type=jnp.float32)
    parts = [out[rr * SUB:(rr + 1) * SUB] for rr in range(4)]
    turned = [pltpu.roll(part, SUB, 1) for part in parts]
    lane = lax.broadcasted_iota(jnp.int32, (SUB, LANES), 1)

    def join(a, b, c, d):
        return jnp.where(lane < SUB, a, jnp.where(lane < 2 * SUB, b, jnp.where(lane < 3 * SUB, c, d)))

    image_re = join(parts[0], turned[1], parts[2], turned[3])
    image_im = join(turned[0], parts[1], turned[2], parts[3])
    return image_re, image_im


def ring_plan():
    return (
        ((3, 0, 0), (1, 0, 1)),
        ((3, 0, 1), (1, 0, 0)),
        ((0, 3, 0), (0, 1, 1)),
        ((0, 3, 1), (0, 1, 0)),
        ((2, 0, 0), (2, 0, 1)),
        ((3, 3, 0), (3, 1, 1), (1, 3, 0), (1, 1, 1)),
        ((0, 2, 0), (0, 2, 1)),
        ((3, 3, 1), (3, 1, 0), (1, 3, 1), (1, 1, 0)),
        ((2, 3, 0), (2, 1, 1)),
        ((3, 2, 0), (3, 2, 1), (1, 2, 0), (1, 2, 1)),
        ((2, 3, 1), (2, 1, 0)),
        ((2, 2, 0), (2, 2, 1)),
    )


def screens_kernel(per_chunk, waits, own_ref, vis_ref, coords_ref, all_ref, image_ref, send_sems, ring_sems, pair_sems,
                   own_sem):
    tile = lax.axis_index("tile")
    core, y, z = tile % 2, tile // 2 % 4, tile // 8

    def chip(who, a, b):
        there_z = (z + who * a + (1 - who) * b) % 4
        there_y = (y + (1 - who) * a + who * b) % 4
        return (there_z * 4 + there_y) * 2 + who

    first_up, first_down = chip(core, 1, 0), chip(core, 3, 0)
    second_up, second_down = chip(core, 0, 1), chip(core, 0, 3)
    pair = (z * 4 + y) * 2 + (1 - core)
    targets = (first_up, first_down, second_up, second_down, pair)

    barrier = pltpu.get_barrier_semaphore()
    for target in targets:
        pl.semaphore_signal(barrier, inc=1, device_id={"tile": target}, device_id_type=pl.DeviceIdType.MESH)
    pl.semaphore_wait(barrier, len(targets))

    half = own_ref.shape[0] // 2
    sent = []

    def place(owner, h):
        return all_ref.at[pl.ds(pl.multiple_of(owner * (2 * half) + h * half, half), half)]

    def unit_index(unit):
        return (unit[0] * 4 + unit[1]) * 2 + unit[2]

    def copy_of(unit, target, sem, number):
        a, b, h = unit
        owner = chip(core, a, b)
        source = own_ref.at[pl.ds(h * half, half)] if (a, b) == (0, 0) else place(owner, h)
        return pltpu.make_async_remote_copy(
            src_ref=source, dst_ref=place(owner, h), send_sem=send_sems.at[number], recv_sem=sem,
            device_id={"tile": target}, device_id_type=pl.DeviceIdType.MESH,
        )

    def push(unit, target, arrives):
        sem = pair_sems.at[unit_index(unit)] if arrives is None else ring_sems.at[unit_index(arrives)]
        copy_of(unit, target, sem, len(sent)).start()
        sent.append(unit)

    def await_ring(unit):
        copy_of(unit, first_up, ring_sems.at[unit_index(unit)], 0).wait_recv()

    def await_pair(unit):
        a, b, h = unit
        owner = chip(1 - core, a, b)
        pltpu.make_async_remote_copy(
            src_ref=place(owner, h), dst_ref=place(owner, h), send_sem=send_sems.at[0],
            recv_sem=pair_sems.at[unit_index(unit)], device_id={"tile": pair}, device_id_type=pl.DeviceIdType.MESH,
        ).wait_recv()

    def forward(unit):
        a, b, h = unit
        if b == 0:
            if (a, h) == (3, 0):
                push(unit, first_up, (2, 0, 0))
            if (a, h) == (1, 1):
                push(unit, first_down, (2, 0, 1))
            up, down = lambda: push(unit, second_up, (a, 3, h)), lambda: push(unit, second_down, (a, 1, h))
            for go in (up, down) if h == 0 else (down, up):
                go()
        elif (b, h) == (3, 0):
            push(unit, second_up, (a, 2, 0))
        elif (b, h) == (1, 1):
            push(unit, second_down, (a, 2, 1))
        push(unit, pair, None)

    push((0, 0, 0), first_up, (3, 0, 0))
    push((0, 0, 1), first_down, (1, 0, 1))
    push((0, 0, 1), first_up, (3, 0, 1))
    push((0, 0, 0), first_down, (1, 0, 0))
    push((0, 0, 0), second_up, (0, 3, 0))
    push((0, 0, 1), second_down, (0, 1, 1))
    push((0, 0, 1), second_up, (0, 3, 1))
    push((0, 0, 0), second_down, (0, 1, 0))
    for h in range(2):
        push((0, 0, h), pair, None)
    local = pltpu.make_async_copy(own_ref, all_ref.at[pl.ds(pl.multiple_of(tile * (2 * half), half), 2 * half)], own_sem)
    local.start()

    first, second = direction_tables()

    def compute(begin, end):
        def step(s, carry):
            image_re, image_im = image_of(coords_ref[s], vis_ref[s], first, second)
            image_ref[s, 0:SUB] = image_re
            image_ref[s, SUB:2 * SUB] = image_im
            return carry

        lax.fori_loop(begin, end, step, 0)

    groups = ring_plan()
    count = vis_ref.shape[0]
    chunks = count // per_chunk

    def chunk(i, carry):
        compute(i * per_chunk, (i + 1) * per_chunk)
        for group, when in zip(groups, waits):
            if when is not None:
                @pl.when(i == when)
                def _():
                    for unit in group:
                        await_ring(unit)
                        forward(unit)
        return carry

    lax.fori_loop(0, chunks, chunk, 0)
    for group, when in zip(groups, waits):
        if when is None:
            for unit in group:
                await_ring(unit)
                forward(unit)
    for a in range(4):
        for b in range(4):
            for h in range(2):
                await_pair((a, b, h))
    for number, unit in enumerate(sent):
        copy_of(unit, pair, pair_sems.at[0], number).wait_send()
    local.wait()


WAITS = (3, 4, 5, 6, 7, 9, 11, 13, None, None, None, None)


def gather_screens(own, visibilities, coords, tile_size):
    count = visibilities.shape[0]
    vmem = pl.BlockSpec(memory_space=pltpu.VMEM)
    own_count = own.shape[0]
    copies = 62
    return pl.pallas_call(
        functools.partial(screens_kernel, 4, WAITS),
        out_shape=(
            jax.ShapeDtypeStruct((own_count * tile_size,) + own.shape[1:], own.dtype),
            jax.ShapeDtypeStruct((count, 2 * SUB, LANES), jnp.float32),
        ),
        in_specs=[vmem, vmem, vmem],
        out_specs=(pl.BlockSpec(memory_space=pl.ANY), vmem),
        scratch_shapes=[
            pltpu.SemaphoreType.DMA((copies,)),
            pltpu.SemaphoreType.DMA((32,)),
            pltpu.SemaphoreType.DMA((32,)),
            pltpu.SemaphoreType.DMA,
        ],
        compiler_params=pltpu.CompilerParams(vmem_limit_bytes=VMEM_LIMIT, collective_id=0, has_side_effects=True),
        name="screens",
    )(own, visibilities, coords)


def sandwich_of(image, near, far):
    def row(array, index):
        return array[index * NJ:(index + 1) * NJ]

    mid_re, mid_im = {}, {}
    for out_row in range(2):
        for inner in range(2):
            total_re = total_im = None
            for first in range(2):
                n_re, n_im = row(near, 2 * first + out_row), row(near, 4 + 2 * first + out_row)
                v_re, v_im = row(image, 2 * first + inner), row(image, 4 + 2 * first + inner)
                re = n_re * v_re + n_im * v_im
                im = n_re * v_im - n_im * v_re
                total_re = re if total_re is None else total_re + re
                total_im = im if total_im is None else total_im + im
            mid_re[out_row, inner], mid_im[out_row, inner] = total_re, total_im
    out_re, out_im = [], []
    for out_row in range(2):
        for out_col in range(2):
            total_re = total_im = None
            for inner in range(2):
                m_re, m_im = mid_re[out_row, inner], mid_im[out_row, inner]
                f_re, f_im = row(far, 2 * inner + out_col), row(far, 4 + 2 * inner + out_col)
                re = m_re * f_re - m_im * f_im
                im = m_re * f_im + m_im * f_re
                total_re = re if total_re is None else total_re + re
                total_im = im if total_im is None else total_im + im
            out_re.append(total_re)
            out_im.append(total_im)
    return out_re, out_im


def fft8(re, im):
    def add(x, y):
        return x[0] + y[0], x[1] + y[1]

    def sub(x, y):
        return x[0] - y[0], x[1] - y[1]

    def turn(x):
        return x[1], -x[0]

    def fft4(x):
        even_add, even_sub = add(x[0], x[2]), sub(x[0], x[2])
        odd_add, odd_sub = add(x[1], x[3]), turn(sub(x[1], x[3]))
        return [add(even_add, odd_add), add(even_sub, odd_sub), sub(even_add, odd_add), sub(even_sub, odd_sub)]

    x = list(zip(re, im))
    even, odd = fft4(x[0::2]), fft4(x[1::2])
    odd = [
        odd[0],
        ((odd[1][0] + odd[1][1]) * ROOT_HALF, (odd[1][1] - odd[1][0]) * ROOT_HALF),
        turn(odd[2]),
        ((odd[3][1] - odd[3][0]) * ROOT_HALF, (-odd[3][0] - odd[3][1]) * ROOT_HALF),
    ]
    out = [add(even[k], odd[k]) for k in range(4)] + [sub(even[k], odd[k]) for k in range(4)]
    return [(-o[0], -o[1]) if k % 2 else o for k, o in enumerate(out)]


def blocks_kernel(count, stations, tile_ids, offsets, image_ref, taper_ref, table_ref, screens, send_ref, meta_ref,
                  near_far, x_re, x_im, y_ref, u_re, u_im, used, sems):
    def fetch(s, which):
        return pltpu.make_async_copy(screens.at[stations[s, which]], near_far.at[s, which], sems.at[s, which])

    def start(s, carry):
        fetch(s, 0).start()
        fetch(s, 1).start()
        return carry

    lax.fori_loop(0, count, start, 0)

    def clear(i, carry):
        used[i] = 0
        return carry

    lax.fori_loop(0, NT, clear, 0)

    def clear_meta(i, carry):
        meta_ref[i] = -1
        return carry

    lax.fori_loop(0, NT * CAP, clear_meta, 0)
    taper = taper_ref[...]

    def sandwich(s, carry):
        fetch(s, 0).wait()
        fetch(s, 1).wait()
        near = near_far[s, 0].astype(jnp.float32)
        far = near_far[s, 1].astype(jnp.float32)
        out_re, out_im = sandwich_of(image_ref[s], near, far)
        for e in range(NCORR):
            rows = pl.ds(pl.multiple_of(s * SUB + e * NJ, NJ), NJ)
            x_re[rows] = out_re[e] * taper
            x_im[rows] = out_im[e] * taper
        return carry

    lax.fori_loop(0, count, sandwich, 0, unroll=2)

    chunk = 16

    def transform(i, carry):
        base = i * (chunk * NJ)
        re = [x_re[pl.ds(base + j, chunk, stride=NJ)] for j in range(NJ)]
        im = [x_im[pl.ds(base + j, chunk, stride=NJ)] for j in range(NJ)]
        rows = pl.ds(pl.multiple_of(i * chunk, chunk), chunk)
        for a8, (y_re, y_im) in enumerate(fft8(re, im)):
            y_ref[a8, rows, 0:LANES] = y_re.astype(jnp.bfloat16)
            y_ref[a8, rows, LANES:2 * LANES] = y_im.astype(jnp.bfloat16)
        return carry

    lax.fori_loop(0, count * NCORR // chunk, transform, 0)

    for a8 in range(NJ):
        out = jnp.dot(y_ref[a8], table_ref[a8], preferred_element_type=jnp.float32)
        u_re[pl.ds(a8, count * NCORR, stride=NJ)] = out[:, 0:LANES]
        u_im[pl.ds(a8, count * NCORR, stride=NJ)] = out[:, LANES:2 * LANES]

    def pack(s, carry):
        tile = tile_ids[s]
        rank = used[tile]
        used[tile] = rank + 1
        slot = tile * CAP + rank
        meta_ref[slot] = offsets[s, 0] * TILE_SIDE + offsets[s, 1]
        target = pl.ds(pl.multiple_of(slot * 2 * NJ, 2 * NJ), 2 * NJ)
        for e in range(NCORR):
            rows = pl.ds(pl.multiple_of(s * SUB + e * NJ, NJ), NJ)
            send_ref[e, target] = jnp.concatenate([u_re[rows], u_im[rows]], axis=0).astype(jnp.bfloat16)
        return carry

    lax.fori_loop(0, count, pack, 0, unroll=2)


def blocks(image, screens, stations, tile_ids, offsets):
    count = image.shape[0]
    vmem = pl.BlockSpec(memory_space=pltpu.VMEM)
    smem = pl.BlockSpec(memory_space=pltpu.SMEM)
    slots = NT * CAP
    points = count * NCORR
    return pl.pallas_call(
        functools.partial(blocks_kernel, count),
        out_shape=(
            jax.ShapeDtypeStruct((NCORR, slots * 2 * NJ, LANES), jnp.bfloat16),
            jax.ShapeDtypeStruct((slots,), jnp.int32),
        ),
        in_specs=[smem, smem, smem, vmem, vmem, vmem, pl.BlockSpec(memory_space=pl.ANY)],
        out_specs=(vmem, smem),
        scratch_shapes=[
            pltpu.VMEM((count, 2, 2 * SUB, LANES), jnp.bfloat16),
            pltpu.VMEM((points * NJ, LANES), jnp.float32),
            pltpu.VMEM((points * NJ, LANES), jnp.float32),
            pltpu.VMEM((NJ, points, 2 * LANES), jnp.bfloat16),
            pltpu.VMEM((points * NJ, LANES), jnp.float32),
            pltpu.VMEM((points * NJ, LANES), jnp.float32),
            pltpu.SMEM((NT,), jnp.int32),
            pltpu.SemaphoreType.DMA((count, 2)),
        ],
        compiler_params=pltpu.CompilerParams(vmem_limit_bytes=VMEM_LIMIT),
        name="blocks",
    )(stations, tile_ids, offsets, image, taper_table(), uv_tables(), screens)


def exchange_kernel(send_ref, meta_ref, recv_ref, table_ref, data_out, data_in, meta_out, meta_in, own_sem, stage):
    corr, tile = lax.axis_index("corr"), lax.axis_index("tile")
    core, y, z = tile % 2, tile // 2 % 4, tile // 8
    devices = recv_ref.shape[0]
    me = corr * (devices // 4) + tile

    def there(k, sign):
        x1 = (corr + sign * (k // 32 % 4) + 4) % 4
        z1 = (z + sign * (k // 8 % 4) + 4) % 4
        y1 = (y + sign * (k // 2 % 4) + 4) % 4
        c1 = (core + k) % 2
        return x1, (z1 * 4 + y1) * 2 + c1

    def device(k):
        x1, t1 = there(k, 1)
        return {"corr": x1, "tile": t1}

    barrier = pltpu.get_barrier_semaphore()

    def greet(k, carry):
        pl.semaphore_signal(barrier, inc=1, device_id=device(k), device_id_type=pl.DeviceIdType.MESH)
        return carry

    lax.fori_loop(1, devices, greet, 0)
    take = pltpu.make_async_copy(send_ref.at[me], stage, own_sem)
    take.start()
    take.wait()
    put = pltpu.make_async_copy(stage, recv_ref.at[me], own_sem)
    put.start()
    put.wait()
    put = pltpu.make_async_copy(meta_ref.at[0], table_ref.at[me], own_sem)
    put.start()
    put.wait()
    pl.semaphore_wait(barrier, devices - 1)

    def data_copy(k):
        x1, t1 = there(k, 1)
        return pltpu.make_async_remote_copy(
            src_ref=send_ref.at[x1 * (devices // 4) + t1], dst_ref=recv_ref.at[me],
            send_sem=data_out.at[k], recv_sem=data_in.at[k],
            device_id={"corr": x1, "tile": t1}, device_id_type=pl.DeviceIdType.MESH,
        )

    def meta_copy(k):
        return pltpu.make_async_remote_copy(
            src_ref=meta_ref.at[0], dst_ref=table_ref.at[me],
            send_sem=meta_out.at[k], recv_sem=meta_in.at[k], device_id=device(k), device_id_type=pl.DeviceIdType.MESH,
        )

    def start(k, carry):
        meta_copy(k).start()
        data_copy(k).start()
        return carry

    lax.fori_loop(1, devices, start, 0)

    def finish(k, carry):
        x1, t1 = there(k, -1)
        source = x1 * (devices // 4) + t1
        pltpu.make_async_remote_copy(
            src_ref=send_ref.at[source], dst_ref=recv_ref.at[source], send_sem=data_out.at[k], recv_sem=data_in.at[k],
            device_id={"corr": x1, "tile": t1}, device_id_type=pl.DeviceIdType.MESH,
        ).wait()
        pltpu.make_async_remote_copy(
            src_ref=meta_ref.at[0], dst_ref=table_ref.at[source], send_sem=meta_out.at[k], recv_sem=meta_in.at[k],
            device_id={"corr": x1, "tile": t1}, device_id_type=pl.DeviceIdType.MESH,
        ).wait()
        return carry

    lax.fori_loop(1, devices, finish, 0)


def exchange(sending, meta):
    devices = sending.shape[0]
    hbm = pl.BlockSpec(memory_space=pl.ANY)
    vmem = pl.BlockSpec(memory_space=pltpu.VMEM)
    sems = pltpu.SemaphoreType.DMA((devices,))
    return pl.pallas_call(
        exchange_kernel,
        out_shape=(
            jax.ShapeDtypeStruct(sending.shape, sending.dtype),
            jax.ShapeDtypeStruct((devices,) + meta.shape[1:], meta.dtype),
        ),
        in_specs=[hbm, vmem],
        out_specs=(hbm, vmem),
        scratch_shapes=[sems, sems, sems, sems, pltpu.SemaphoreType.DMA, pltpu.VMEM(sending.shape[1:], sending.dtype)],
        compiler_params=pltpu.CompilerParams(vmem_limit_bytes=VMEM_LIMIT, collective_id=1, has_side_effects=True),
        name="exchange",
    )(sending, meta)


def gather_kernel(sources, per_owner, table, recv_ref, out_ref, acc):
    acc[...] = jnp.zeros_like(acc)
    lane = lax.broadcasted_iota(jnp.int32, (NJ, LANES), 1)
    slots = per_owner * CAP
    own = lax.axis_index("tile") * slots

    def step(src, carry):
        for slot in range(slots):
            place = table[src, own + slot]
            valid = place >= 0
            row0 = jnp.where(valid, place >> 7, 0)
            col0 = jnp.where(valid, place & (TILE_SIDE - 1), 0)
            begin = jnp.where(valid, row0, 2 * LANES)
            inside = (lane >= begin) & (lane < begin + SUB)
            block = recv_ref[src, slot * 2 * NJ:(slot + 1) * 2 * NJ].astype(jnp.float32)
            for part in range(2):
                data = block[part * NJ:(part + 1) * NJ]
                moved = []
                for a4 in range(4):
                    shift = (row0 + (LANES - a4 * SUB)) & (LANES - 1)
                    moved.append(jnp.where(inside, pltpu.roll(data, shift, 1), 0.0))
                rows = pl.ds(col0, SUB)
                acc[slot, part, rows] = acc[slot, part, rows] + jnp.concatenate(moved, axis=0)
        return carry

    lax.fori_loop(0, sources, step, 0, unroll=2)
    for tile in range(per_owner):
        for part in range(2):
            total = acc[tile * CAP, part]
            for rank in range(1, CAP):
                total = total + acc[tile * CAP + rank, part]
            out_ref[tile, part] = total.T


def gather_blocks(received, meta, per_owner):
    sources = received.shape[0]
    vmem = pl.BlockSpec(memory_space=pltpu.VMEM)
    return pl.pallas_call(
        functools.partial(gather_kernel, sources, per_owner),
        out_shape=jax.ShapeDtypeStruct((per_owner, 2, TILE_SIDE, TILE_SIDE), jnp.float32),
        in_specs=[pl.BlockSpec(memory_space=pltpu.SMEM), vmem],
        out_specs=vmem,
        scratch_shapes=[pltpu.VMEM((per_owner * CAP, 2, TILE_SIDE, TILE_SIDE), jnp.float32)],
        compiler_params=pltpu.CompilerParams(vmem_limit_bytes=VMEM_LIMIT),
        name="accumulate",
    )(meta, received)


def per_device(visibilities, coords, stations, tile_ids, offsets, screens):
    tile_size = lax.axis_size("tile")
    per_owner = NT // tile_size
    own = screens.reshape(screens.shape[0], 2 * SUB, LANES)
    all_screens, image = gather_screens(own, visibilities, coords, tile_size)
    sending, meta = blocks(image, all_screens, stations, tile_ids[:, 0], offsets)
    rows = per_owner * CAP * 2 * NJ
    received, table = exchange(sending.reshape(NCORR * tile_size, rows, LANES), meta.reshape(1, 1, NT * CAP))
    return gather_blocks(received, table.reshape(-1, NT * CAP), per_owner)[None]


def solution(mesh):
    return jax.shard_map(
        per_device,
        mesh=mesh,
        in_specs=(
            P(("corr", "tile"), None, None),
            P(("corr", "tile"), None, None),
            P(("corr", "tile"), None),
            P(("corr", "tile"), None),
            P(("corr", "tile"), None),
            P("tile", None, None),
        ),
        out_specs=P("corr", "tile", None, None, None),
        check_vma=False,
    )
```

```python
import functools
import math

import jax
import jax.numpy as jnp
import numpy as np
from jax import lax
from jax.experimental import pallas as pl
from jax.experimental.pallas import tpu as pltpu
from jax.sharding import PartitionSpec as P

SUB = 32
NT = 64
TILE_SIDE = 128
NVIS = 256
PIX = 1024
NCORR = 4
CAP = 2
NJ = 8
LANES = 128
SIN_POLY = (3.141592579805584, -5.167706866167941, 2.550031193519298, -0.5980441939119835, 0.07721838615698538)
COS_POLY = (0.9999999532476082, -4.934792830619647, 4.058411352862557, -1.3318765680805114, 0.2196896110968953)
ROOT_HALF = math.sqrt(0.5)
VMEM_LIMIT = 60 * 1024 * 1024


def uv_tables():
    rr = np.arange(4)[:, None, None, None]
    c = np.arange(SUB)[None, :, None, None]
    a4 = np.arange(4)[None, None, :, None]
    d = np.arange(SUB)[None, None, None, :]
    half = SUB // 2
    tables = []
    for a8 in range(NJ):
        turns = (rr * (a8 + 8 * a4 - half) + (c - half) * (d - half)) % SUB
        angle = (-2.0 * np.pi / SUB) * turns.reshape(LANES, LANES)
        re, im = np.cos(angle) / SUB, np.sin(angle) / SUB
        tables.append(np.block([[re, im], [-im, re]]))
    return jnp.asarray(np.stack(tables), jnp.bfloat16)


def taper_table():
    pos = (np.arange(SUB) - SUB // 2 + 0.5) / (SUB // 2)
    edge = 1.0 - 0.8 * pos * pos
    return jnp.asarray((edge[:, None] * edge[None, :] / NVIS).reshape(NJ, LANES), jnp.float32)


def poly(square, coefficients):
    total = jnp.full_like(square, coefficients[-1])
    for coefficient in coefficients[-2::-1]:
        total = total * square + coefficient
    return total


def cos_sin_turns(turns):
    rest = turns - jnp.round(turns)
    square = rest * rest
    sine = rest * poly(square, SIN_POLY)
    cosine = poly(square, COS_POLY)
    twice = sine + sine
    return 1.0 - twice * sine, twice * cosine


def direction_tables():
    row = lax.broadcasted_iota(jnp.int32, (2 * SUB, NVIS), 0)
    r = (row % NJ) * 4 + row // NJ
    place = jnp.where(row < SUB, r, row - SUB)
    first = (place - SUB // 2).astype(jnp.float32) * (1.0 / SUB)
    return first, -0.5 * first * first


def image_of(u, v, w, vis, first, second):
    linear = jnp.concatenate([u * first[:SUB], v * first[SUB:]], axis=0)
    cosine, sine = cos_sin_turns(linear + w * second)
    row_re, row_im = cosine[:SUB], sine[:SUB]
    col_re, col_im = cosine[SUB:], sine[SUB:]
    vis = vis.astype(jnp.float32)
    lhs = []
    for rr in range(4):
        a_re, a_im = row_re[rr * NJ:(rr + 1) * NJ], row_im[rr * NJ:(rr + 1) * NJ]
        part_re, part_im = [], []
        for e in range(NCORR):
            v_re, v_im = vis[e:e + 1], vis[NCORR + e:NCORR + e + 1]
            part_re.append(v_re * a_re - v_im * a_im)
            part_im.append(v_re * a_im + v_im * a_re)
        lhs.append(jnp.concatenate([jnp.concatenate(part_re, axis=0), jnp.concatenate(part_im, axis=0)], axis=1))
    lhs = jnp.concatenate(lhs, axis=0).astype(jnp.bfloat16)
    upper = jnp.concatenate([col_re, -col_im], axis=1)
    lower = jnp.concatenate([col_im, col_re], axis=1)
    rhs = jnp.concatenate([upper, lower, upper, lower], axis=0).astype(jnp.bfloat16)
    out = lax.dot_general(lhs, rhs, (((1,), (1,)), ((), ())), preferred_element_type=jnp.float32)
    parts = [out[rr * SUB:(rr + 1) * SUB] for rr in range(4)]
    turned = [pltpu.roll(part, SUB, 1) for part in parts]
    lane = lax.broadcasted_iota(jnp.int32, (SUB, LANES), 1)

    def join(a, b, c, d):
        return jnp.where(lane < SUB, a, jnp.where(lane < 2 * SUB, b, jnp.where(lane < 3 * SUB, c, d)))

    image_re = join(parts[0], turned[1], parts[2], turned[3])
    image_im = join(turned[0], parts[1], turned[2], parts[3])
    return image_re, image_im


def ring_plan():
    return (
        ((3, 0, 0), (1, 0, 1)),
        ((3, 0, 1), (1, 0, 0)),
        ((0, 3, 0), (0, 1, 1)),
        ((0, 3, 1), (0, 1, 0)),
        ((2, 0, 0), (2, 0, 1)),
        ((3, 3, 0), (3, 1, 1), (1, 3, 0), (1, 1, 1)),
        ((0, 2, 0), (0, 2, 1)),
        ((3, 3, 1), (3, 1, 0), (1, 3, 1), (1, 1, 0)),
        ((2, 3, 0), (2, 1, 1)),
        ((3, 2, 0), (3, 2, 1), (1, 2, 0), (1, 2, 1)),
        ((2, 3, 1), (2, 1, 0)),
        ((2, 2, 0), (2, 2, 1)),
    )


def slot_row(tiles, rows, cols):
    count, slots = tiles.shape[1], NT * CAP
    slot = lax.broadcasted_iota(jnp.int32, (slots, count), 0)
    named = tiles == (slot >> 1)
    earlier = lax.broadcasted_iota(jnp.int32, (count, count), 0) < lax.broadcasted_iota(jnp.int32, (count, count), 1)
    rank = jnp.dot(
        named.astype(jnp.float32).astype(jnp.bfloat16), earlier.astype(jnp.float32).astype(jnp.bfloat16),
        preferred_element_type=jnp.float32,
    )
    taken = named & (rank == (slot & 1).astype(jnp.float32))
    value = (rows * TILE_SIDE + cols + 1).astype(jnp.float32)
    column = jnp.sum(jnp.where(taken, value, 0.0), axis=1, keepdims=True)
    shape = (slots, slots)
    diagonal = lax.broadcasted_iota(jnp.int32, shape, 0) == lax.broadcasted_iota(jnp.int32, shape, 1)
    line = jnp.sum(jnp.where(diagonal, jnp.broadcast_to(column, shape), 0.0), axis=0, keepdims=True)
    return line.astype(jnp.int32) - 1


def screens_kernel(per_chunk, waits, own_ref, vis_ref, coords_ref, tiles_ref, offsets_ref, all_ref, image_ref, table_ref,
                   send_sems, ring_sems, pair_sems, own_sem, plane_out, plane_in, axis_out, axis_in):
    corr, tile = lax.axis_index("corr"), lax.axis_index("tile")
    planes, plane = lax.axis_size("corr"), lax.axis_size("tile")
    me = corr * plane + tile
    core, y, z = tile % 2, tile // 2 % 4, tile // 8

    def chip(who, a, b):
        there_z = (z + who * a + (1 - who) * b) % 4
        there_y = (y + (1 - who) * a + who * b) % 4
        return (there_z * 4 + there_y) * 2 + who

    first_up, first_down = chip(core, 1, 0), chip(core, 3, 0)
    second_up, second_down = chip(core, 0, 1), chip(core, 0, 3)
    pair = (z * 4 + y) * 2 + (1 - core)
    barrier = pltpu.get_barrier_semaphore()

    def in_plane(t):
        return {"tile": (tile + t) % plane}

    def along(t):
        return {"corr": (corr + t) % planes}

    def greet(t, carry):
        pl.semaphore_signal(barrier, inc=1, device_id=in_plane(t), device_id_type=pl.DeviceIdType.MESH)
        return carry

    lax.fori_loop(1, plane, greet, 0)
    for t in range(1, planes):
        pl.semaphore_signal(barrier, inc=1, device_id=along(t), device_id_type=pl.DeviceIdType.MESH)
    table_ref[pl.ds(me, 1)] = slot_row(tiles_ref[...], offsets_ref[0:1], offsets_ref[1:2])[None]
    pl.semaphore_wait(barrier, plane + planes - 2)

    def plane_copy(t, source):
        return pltpu.make_async_remote_copy(
            src_ref=table_ref.at[source], dst_ref=table_ref.at[source], send_sem=plane_out.at[t], recv_sem=plane_in.at[t],
            device_id=in_plane(t), device_id_type=pl.DeviceIdType.MESH,
        )

    def axis_copy(t, source):
        rows = table_ref.at[pl.ds(source * plane, plane)]
        return pltpu.make_async_remote_copy(
            src_ref=rows, dst_ref=rows, send_sem=axis_out.at[t], recv_sem=axis_in.at[t],
            device_id=along(t), device_id_type=pl.DeviceIdType.MESH,
        )

    def plane_start(t, carry):
        plane_copy(t, me).start()
        return carry

    def plane_wait(t, carry):
        plane_copy(t, corr * plane + (tile + plane - t) % plane).wait()
        return carry

    half = own_ref.shape[0] // 2
    sent = []

    def place(owner, h):
        return all_ref.at[pl.ds(pl.multiple_of(owner * (2 * half) + h * half, half), half)]

    def unit_index(unit):
        return (unit[0] * 4 + unit[1]) * 2 + unit[2]

    def copy_of(unit, target, sem, number):
        a, b, h = unit
        owner = chip(core, a, b)
        source = own_ref.at[pl.ds(h * half, half)] if (a, b) == (0, 0) else place(owner, h)
        return pltpu.make_async_remote_copy(
            src_ref=source, dst_ref=place(owner, h), send_sem=send_sems.at[number], recv_sem=sem,
            device_id={"tile": target}, device_id_type=pl.DeviceIdType.MESH,
        )

    def push(unit, target, arrives):
        sem = pair_sems.at[unit_index(unit)] if arrives is None else ring_sems.at[unit_index(arrives)]
        copy_of(unit, target, sem, len(sent)).start()
        sent.append(unit)

    def await_ring(unit):
        copy_of(unit, first_up, ring_sems.at[unit_index(unit)], 0).wait_recv()

    def await_pair(unit):
        a, b, h = unit
        owner = chip(1 - core, a, b)
        pltpu.make_async_remote_copy(
            src_ref=place(owner, h), dst_ref=place(owner, h), send_sem=send_sems.at[0],
            recv_sem=pair_sems.at[unit_index(unit)], device_id={"tile": pair}, device_id_type=pl.DeviceIdType.MESH,
        ).wait_recv()

    def forward(unit):
        a, b, h = unit
        if b == 0:
            if (a, h) == (3, 0):
                push(unit, first_up, (2, 0, 0))
            if (a, h) == (1, 1):
                push(unit, first_down, (2, 0, 1))
            up, down = lambda: push(unit, second_up, (a, 3, h)), lambda: push(unit, second_down, (a, 1, h))
            for go in (up, down) if h == 0 else (down, up):
                go()
        elif (b, h) == (3, 0):
            push(unit, second_up, (a, 2, 0))
        elif (b, h) == (1, 1):
            push(unit, second_down, (a, 2, 1))
        push(unit, pair, None)

    push((0, 0, 0), first_up, (3, 0, 0))
    push((0, 0, 1), first_down, (1, 0, 1))
    push((0, 0, 1), first_up, (3, 0, 1))
    push((0, 0, 0), first_down, (1, 0, 0))
    push((0, 0, 0), second_up, (0, 3, 0))
    push((0, 0, 1), second_down, (0, 1, 1))
    push((0, 0, 1), second_up, (0, 3, 1))
    push((0, 0, 0), second_down, (0, 1, 0))
    for h in range(2):
        push((0, 0, h), pair, None)
    local = pltpu.make_async_copy(own_ref, all_ref.at[pl.ds(pl.multiple_of(tile * (2 * half), half), 2 * half)], own_sem)
    local.start()

    first, second = direction_tables()

    def compute(begin, end):
        def step(s, carry):
            u, v, w = (coords_ref[axis, pl.ds(s, 1)] for axis in range(3))
            image_re, image_im = image_of(u, v, w, vis_ref[s], first, second)
            image_ref[s, 0:SUB] = image_re
            image_ref[s, SUB:2 * SUB] = image_im
            return carry

        lax.fori_loop(begin, end, step, 0)

    groups = ring_plan()
    count = vis_ref.shape[0]
    chunks = count // per_chunk

    def chunk(i, carry):
        compute(i * per_chunk, (i + 1) * per_chunk)

        @pl.when(i == 0)
        def _():
            lax.fori_loop(1, plane, plane_start, 0)

        @pl.when(i == chunks - 4)
        def _():
            lax.fori_loop(1, plane, plane_wait, 0)
            for t in range(1, planes):
                axis_copy(t, corr).start()

        for group, when in zip(groups, waits):
            if when is not None:
                @pl.when(i == when)
                def _():
                    for unit in group:
                        await_ring(unit)
                        forward(unit)
        return carry

    lax.fori_loop(0, chunks, chunk, 0)
    for group, when in zip(groups, waits):
        if when is None:
            for unit in group:
                await_ring(unit)
                forward(unit)
    for a in range(4):
        for b in range(4):
            for h in range(2):
                await_pair((a, b, h))
    for number, unit in enumerate(sent):
        copy_of(unit, pair, pair_sems.at[0], number).wait_send()
    for t in range(1, planes):
        axis_copy(t, (corr + planes - t) % planes).wait()
    local.wait()


WAITS = (3, 4, 5, 6, 7, 9, 11, 13, None, None, None, None)


def gather_screens(own, visibilities, coords, tiles, offsets, devices, tile_size):
    count = visibilities.shape[0]
    vmem = pl.BlockSpec(memory_space=pltpu.VMEM)
    own_count = own.shape[0]
    copies = 62
    return pl.pallas_call(
        functools.partial(screens_kernel, 4, WAITS),
        out_shape=(
            jax.ShapeDtypeStruct((own_count * tile_size,) + own.shape[1:], own.dtype),
            jax.ShapeDtypeStruct((count, 2 * SUB, LANES), jnp.float32),
            jax.ShapeDtypeStruct((devices, 1, NT * CAP), jnp.int32),
        ),
        in_specs=[vmem] * 5,
        out_specs=(pl.BlockSpec(memory_space=pl.ANY), vmem, vmem),
        scratch_shapes=[
            pltpu.SemaphoreType.DMA((copies,)),
            pltpu.SemaphoreType.DMA((32,)),
            pltpu.SemaphoreType.DMA((32,)),
            pltpu.SemaphoreType.DMA,
            pltpu.SemaphoreType.DMA((tile_size,)),
            pltpu.SemaphoreType.DMA((tile_size,)),
            pltpu.SemaphoreType.DMA((devices // tile_size,)),
            pltpu.SemaphoreType.DMA((devices // tile_size,)),
        ],
        compiler_params=pltpu.CompilerParams(vmem_limit_bytes=VMEM_LIMIT, collective_id=0, has_side_effects=True),
        name="screens",
    )(own, visibilities, coords, tiles, offsets)


def sandwich_of(image, near, far):
    def row(array, index):
        return array[index * NJ:(index + 1) * NJ]

    mid_re, mid_im = {}, {}
    for out_row in range(2):
        for inner in range(2):
            total_re = total_im = None
            for first in range(2):
                n_re, n_im = row(near, 2 * first + out_row), row(near, 4 + 2 * first + out_row)
                v_re, v_im = row(image, 2 * first + inner), row(image, 4 + 2 * first + inner)
                re = n_re * v_re + n_im * v_im
                im = n_re * v_im - n_im * v_re
                total_re = re if total_re is None else total_re + re
                total_im = im if total_im is None else total_im + im
            mid_re[out_row, inner], mid_im[out_row, inner] = total_re, total_im
    out_re, out_im = [], []
    for out_row in range(2):
        for out_col in range(2):
            total_re = total_im = None
            for inner in range(2):
                m_re, m_im = mid_re[out_row, inner], mid_im[out_row, inner]
                f_re, f_im = row(far, 2 * inner + out_col), row(far, 4 + 2 * inner + out_col)
                re = m_re * f_re - m_im * f_im
                im = m_re * f_im + m_im * f_re
                total_re = re if total_re is None else total_re + re
                total_im = im if total_im is None else total_im + im
            out_re.append(total_re)
            out_im.append(total_im)
    return out_re, out_im


def fft8(re, im):
    def add(x, y):
        return x[0] + y[0], x[1] + y[1]

    def sub(x, y):
        return x[0] - y[0], x[1] - y[1]

    def turn(x):
        return x[1], -x[0]

    def fft4(x):
        even_add, even_sub = add(x[0], x[2]), sub(x[0], x[2])
        odd_add, odd_sub = add(x[1], x[3]), turn(sub(x[1], x[3]))
        return [add(even_add, odd_add), add(even_sub, odd_sub), sub(even_add, odd_add), sub(even_sub, odd_sub)]

    x = list(zip(re, im))
    even, odd = fft4(x[0::2]), fft4(x[1::2])
    odd = [
        odd[0],
        ((odd[1][0] + odd[1][1]) * ROOT_HALF, (odd[1][1] - odd[1][0]) * ROOT_HALF),
        turn(odd[2]),
        ((odd[3][1] - odd[3][0]) * ROOT_HALF, (-odd[3][0] - odd[3][1]) * ROOT_HALF),
    ]
    out = [add(even[k], odd[k]) for k in range(4)] + [sub(even[k], odd[k]) for k in range(4)]
    return [(-o[0], -o[1]) if k % 2 else o for k, o in enumerate(out)]


def blocks_kernel(count, stations, tile_ids, image_ref, taper_ref, table_ref, screens, send_ref, near_far, x_re,
                  x_im, y_ref, u_re, u_im, used, sems):
    def fetch(s, which):
        return pltpu.make_async_copy(screens.at[stations[which, s]], near_far.at[s, which], sems.at[s, which])

    def start(s, carry):
        fetch(s, 0).start()
        fetch(s, 1).start()
        return carry

    lax.fori_loop(0, count, start, 0)

    def clear(i, carry):
        used[i] = 0
        return carry

    lax.fori_loop(0, NT, clear, 0)

    taper = taper_ref[...]

    def sandwich(s, carry):
        fetch(s, 0).wait()
        fetch(s, 1).wait()
        near = near_far[s, 0].astype(jnp.float32)
        far = near_far[s, 1].astype(jnp.float32)
        out_re, out_im = sandwich_of(image_ref[s], near, far)
        for e in range(NCORR):
            rows = pl.ds(pl.multiple_of(s * SUB + e * NJ, NJ), NJ)
            x_re[rows] = out_re[e] * taper
            x_im[rows] = out_im[e] * taper
        return carry

    lax.fori_loop(0, count, sandwich, 0, unroll=2)

    chunk = 16

    def transform(i, carry):
        base = i * (chunk * NJ)
        re = [x_re[pl.ds(base + j, chunk, stride=NJ)] for j in range(NJ)]
        im = [x_im[pl.ds(base + j, chunk, stride=NJ)] for j in range(NJ)]
        rows = pl.ds(pl.multiple_of(i * chunk, chunk), chunk)
        for a8, (y_re, y_im) in enumerate(fft8(re, im)):
            y_ref[a8, rows, 0:LANES] = y_re.astype(jnp.bfloat16)
            y_ref[a8, rows, LANES:2 * LANES] = y_im.astype(jnp.bfloat16)
        return carry

    lax.fori_loop(0, count * NCORR // chunk, transform, 0)

    for a8 in range(NJ):
        out = jnp.dot(y_ref[a8], table_ref[a8], preferred_element_type=jnp.float32)
        u_re[pl.ds(a8, count * NCORR, stride=NJ)] = out[:, 0:LANES]
        u_im[pl.ds(a8, count * NCORR, stride=NJ)] = out[:, LANES:2 * LANES]

    def pack(s, carry):
        tile = tile_ids[s]
        rank = used[tile]
        used[tile] = rank + 1
        slot = tile * CAP + rank
        target = pl.ds(pl.multiple_of(slot * 2 * NJ, 2 * NJ), 2 * NJ)
        for e in range(NCORR):
            rows = pl.ds(pl.multiple_of(s * SUB + e * NJ, NJ), NJ)
            send_ref[e, target] = jnp.concatenate([u_re[rows], u_im[rows]], axis=0).astype(jnp.bfloat16)
        return carry

    lax.fori_loop(0, count, pack, 0, unroll=2)


def blocks(image, screens, stations, tile_ids):
    count = image.shape[0]
    vmem = pl.BlockSpec(memory_space=pltpu.VMEM)
    smem = pl.BlockSpec(memory_space=pltpu.SMEM)
    slots = NT * CAP
    points = count * NCORR
    return pl.pallas_call(
        functools.partial(blocks_kernel, count),
        out_shape=jax.ShapeDtypeStruct((NCORR, slots * 2 * NJ, LANES), jnp.bfloat16),
        in_specs=[smem, smem, vmem, vmem, vmem, pl.BlockSpec(memory_space=pl.ANY)],
        out_specs=vmem,
        scratch_shapes=[
            pltpu.VMEM((count, 2, 2 * SUB, LANES), jnp.bfloat16),
            pltpu.VMEM((points * NJ, LANES), jnp.float32),
            pltpu.VMEM((points * NJ, LANES), jnp.float32),
            pltpu.VMEM((NJ, points, 2 * LANES), jnp.bfloat16),
            pltpu.VMEM((points * NJ, LANES), jnp.float32),
            pltpu.VMEM((points * NJ, LANES), jnp.float32),
            pltpu.SMEM((NT,), jnp.int32),
            pltpu.SemaphoreType.DMA((count, 2)),
        ],
        compiler_params=pltpu.CompilerParams(vmem_limit_bytes=VMEM_LIMIT),
        name="blocks",
    )(stations, tile_ids, image, taper_table(), uv_tables(), screens)


def exchange_kernel(per_owner, table, send_ref, out_ref, recv, moved, acc, data_out, data_in, own_sem):
    corr, tile = lax.axis_index("corr"), lax.axis_index("tile")
    planes, plane = lax.axis_size("corr"), lax.axis_size("tile")
    devices = planes * plane
    core, y, z = tile % 2, tile // 2 % 4, tile // 8
    slots = per_owner * CAP

    def there(k, sign):
        d = k * ORDER % devices
        x1 = (corr + sign * (d // 32 % 4) + 4) % 4
        z1 = (z + sign * (d // 8 % 4) + 4) % 4
        y1 = (y + sign * (d // 2 % 4) + 4) % 4
        return x1, (z1 * 4 + y1) * 2 + (core + d) % 2

    barrier = pltpu.get_barrier_semaphore()

    def greet(k, carry):
        x1, t1 = there(k, -1)
        pl.semaphore_signal(barrier, inc=1, device_id={"corr": x1, "tile": t1}, device_id_type=pl.DeviceIdType.MESH)
        return carry

    lax.fori_loop(1, devices, greet, 0)
    own = pltpu.make_async_copy(send_ref.at[corr * plane + tile], recv.at[0], own_sem)
    own.start()
    acc[...] = jnp.zeros_like(acc)
    pl.semaphore_wait(barrier, devices - 1)

    def copy_of(k):
        x1, t1 = there(k, 1)
        return pltpu.make_async_remote_copy(
            src_ref=send_ref.at[x1 * plane + t1], dst_ref=recv.at[k], send_sem=data_out.at[k], recv_sem=data_in.at[k],
            device_id={"corr": x1, "tile": t1}, device_id_type=pl.DeviceIdType.MESH,
        )

    def start(k, carry):
        copy_of(k).start()
        return carry

    lax.fori_loop(1, devices, start, 0)
    own.wait()

    lane = lax.broadcasted_iota(jnp.int32, (NJ, LANES), 1)
    batch = 4
    depth = batch * CAP * SUB
    target_lane = lax.broadcasted_iota(jnp.int32, (1, depth), 1)
    target_row = lax.broadcasted_iota(jnp.int32, (TILE_SIDE, depth), 0)

    def group(g, carry):
        firsts = [jnp.zeros((1, depth), jnp.int32) for _ in range(per_owner)]
        for i in range(batch):
            k = g * batch + i

            @pl.when(k > 0)
            def _():
                copy_of(k).wait()

            x1, t1 = there(k, -1)
            source = x1 * plane + t1
            for slot in range(slots):
                place = table[source, tile * slots + slot]
                row0, col0 = place >> 7, place & (TILE_SIDE - 1)
                begin = jnp.where(place >= 0, row0, 2 * LANES)
                inside = (lane >= begin) & (lane < begin + SUB)
                block = recv[k, slot * 2 * NJ:(slot + 1) * 2 * NJ].astype(jnp.float32)
                number = i * CAP + slot % CAP
                for part in range(2):
                    data = block[part * NJ:(part + 1) * NJ]
                    rolled = []
                    for a4 in range(4):
                        shift = (row0 + (LANES - a4 * SUB)) & (LANES - 1)
                        rolled.append(jnp.where(inside, pltpu.roll(data, shift, 1), 0.0))
                    rolled = jnp.concatenate(rolled, axis=0).astype(jnp.bfloat16)
                    moved[slot // CAP, number * SUB:(number + 1) * SUB, part * LANES:(part + 1) * LANES] = rolled
                firsts[slot // CAP] = jnp.where(target_lane >= number * SUB, col0 - number * SUB, firsts[slot // CAP])
        for own_tile in range(per_owner):
            select = (target_row == firsts[own_tile] + target_lane).astype(jnp.float32).astype(jnp.bfloat16)
            acc[own_tile] += jnp.dot(select, moved[own_tile], preferred_element_type=jnp.float32)
        return carry

    lax.fori_loop(0, devices // batch, group, 0)
    for own_tile in range(per_owner):
        for part in range(2):
            out_ref[own_tile, part] = acc[own_tile, :, part * LANES:(part + 1) * LANES].T


ORDER = 37


def exchange(sending, table, per_owner):
    devices = sending.shape[0]
    sems = pltpu.SemaphoreType.DMA((devices,))
    return pl.pallas_call(
        functools.partial(exchange_kernel, per_owner),
        out_shape=jax.ShapeDtypeStruct((per_owner, 2, TILE_SIDE, TILE_SIDE), jnp.float32),
        in_specs=[pl.BlockSpec(memory_space=pltpu.SMEM), pl.BlockSpec(memory_space=pl.ANY)],
        out_specs=pl.BlockSpec(memory_space=pltpu.VMEM),
        scratch_shapes=[
            pltpu.VMEM(sending.shape, sending.dtype),
            pltpu.VMEM((per_owner, 4 * CAP * SUB, 2 * LANES), jnp.bfloat16),
            pltpu.VMEM((per_owner, TILE_SIDE, 2 * LANES), jnp.float32),
            sems,
            sems,
            pltpu.SemaphoreType.DMA,
        ],
        compiler_params=pltpu.CompilerParams(vmem_limit_bytes=VMEM_LIMIT, collective_id=1, has_side_effects=True),
        name="exchange",
    )(table, sending)


def per_device(visibilities, coords, stations, tile_ids, offsets, screens):
    tile_size = lax.axis_size("tile")
    devices = lax.axis_size("corr") * tile_size
    per_owner = NT // tile_size
    own = screens.reshape(screens.shape[0], 2 * SUB, LANES)
    all_screens, image, table = gather_screens(
        own, visibilities, coords.transpose(1, 0, 2), tile_ids.T, offsets.T, devices, tile_size
    )
    sending = blocks(image, all_screens, stations.T, tile_ids[:, 0])
    sending = sending.reshape(devices, per_owner * CAP * 2 * NJ, LANES)
    return exchange(sending, table.reshape(devices, NT * CAP), per_owner)[None]


def solution(mesh):
    return jax.shard_map(
        per_device,
        mesh=mesh,
        in_specs=(
            P(("corr", "tile"), None, None),
            P(("corr", "tile"), None, None),
            P(("corr", "tile"), None),
            P(("corr", "tile"), None),
            P(("corr", "tile"), None),
            P("tile", None, None),
        ),
        out_specs=P("corr", "tile", None, None, None),
        check_vma=False,
    )
```

```python
import functools
import math

import jax
import jax.numpy as jnp
import numpy as np
from jax import lax
from jax.experimental import pallas as pl
from jax.experimental.pallas import tpu as pltpu
from jax.sharding import PartitionSpec as P

SUB = 32
NT = 64
TILE_SIDE = 128
NVIS = 256
PIX = 1024
NCORR = 4
CAP = 2
NJ = 8
LANES = 128
SIN_POLY = (3.141592579805584, -5.167706866167941, 2.550031193519298, -0.5980441939119835, 0.07721838615698538)
COS_POLY = (0.9999999532476082, -4.934792830619647, 4.058411352862557, -1.3318765680805114, 0.2196896110968953)
ROOT_HALF = math.sqrt(0.5)
VMEM_LIMIT = 60 * 1024 * 1024


def uv_tables():
    rr = np.arange(4)[:, None, None, None]
    c = np.arange(SUB)[None, :, None, None]
    a4 = np.arange(4)[None, None, :, None]
    d = np.arange(SUB)[None, None, None, :]
    half = SUB // 2
    tables = []
    for a8 in range(NJ):
        turns = (rr * (a8 + 8 * a4 - half) + (c - half) * (d - half)) % SUB
        angle = (-2.0 * np.pi / SUB) * turns.reshape(LANES, LANES)
        re, im = np.cos(angle) / SUB, np.sin(angle) / SUB
        tables.append(np.block([[re, im], [-im, re]]))
    return jnp.asarray(np.stack(tables), jnp.bfloat16)


def taper_table():
    pos = (np.arange(SUB) - SUB // 2 + 0.5) / (SUB // 2)
    edge = 1.0 - 0.8 * pos * pos
    return jnp.asarray((edge[:, None] * edge[None, :] / NVIS).reshape(NJ, LANES), jnp.float32)


def poly(square, coefficients):
    total = jnp.full_like(square, coefficients[-1])
    for coefficient in coefficients[-2::-1]:
        total = total * square + coefficient
    return total


def cos_sin_turns(turns):
    rest = turns - jnp.round(turns)
    square = rest * rest
    sine = rest * poly(square, SIN_POLY)
    cosine = poly(square, COS_POLY)
    twice = sine + sine
    return 1.0 - twice * sine, twice * cosine


def direction_tables():
    row = lax.broadcasted_iota(jnp.int32, (2 * SUB, NVIS), 0)
    r = (row % NJ) * 4 + row // NJ
    place = jnp.where(row < SUB, r, row - SUB)
    first = (place - SUB // 2).astype(jnp.float32) * (1.0 / SUB)
    return first, -0.5 * first * first


def image_of(u, v, w, vis, first, second):
    linear = jnp.concatenate([u * first[:SUB], v * first[SUB:]], axis=0)
    cosine, sine = cos_sin_turns(linear + w * second)
    row_re, row_im = cosine[:SUB], sine[:SUB]
    col_re, col_im = cosine[SUB:], sine[SUB:]
    vis = vis.astype(jnp.float32)
    lhs = []
    for rr in range(4):
        a_re, a_im = row_re[rr * NJ:(rr + 1) * NJ], row_im[rr * NJ:(rr + 1) * NJ]
        part_re, part_im = [], []
        for e in range(NCORR):
            v_re, v_im = vis[e:e + 1], vis[NCORR + e:NCORR + e + 1]
            part_re.append(v_re * a_re - v_im * a_im)
            part_im.append(v_re * a_im + v_im * a_re)
        lhs.append(jnp.concatenate([jnp.concatenate(part_re, axis=0), jnp.concatenate(part_im, axis=0)], axis=1))
    lhs = jnp.concatenate(lhs, axis=0).astype(jnp.bfloat16)
    upper = jnp.concatenate([col_re, -col_im], axis=1)
    lower = jnp.concatenate([col_im, col_re], axis=1)
    rhs = jnp.concatenate([upper, lower, upper, lower], axis=0).astype(jnp.bfloat16)
    out = lax.dot_general(lhs, rhs, (((1,), (1,)), ((), ())), preferred_element_type=jnp.float32)
    parts = [out[rr * SUB:(rr + 1) * SUB] for rr in range(4)]
    turned = [pltpu.roll(part, SUB, 1) for part in parts]
    lane = lax.broadcasted_iota(jnp.int32, (SUB, LANES), 1)

    def join(a, b, c, d):
        return jnp.where(lane < SUB, a, jnp.where(lane < 2 * SUB, b, jnp.where(lane < 3 * SUB, c, d)))

    image_re = join(parts[0], turned[1], parts[2], turned[3])
    image_im = join(turned[0], parts[1], turned[2], parts[3])
    return image_re, image_im


def ring_plan():
    return (
        ((3, 0, 0), (1, 0, 1)),
        ((3, 0, 1), (1, 0, 0)),
        ((0, 3, 0), (0, 1, 1)),
        ((0, 3, 1), (0, 1, 0)),
        ((2, 0, 0), (2, 0, 1)),
        ((3, 3, 0), (3, 1, 1), (1, 3, 0), (1, 1, 1)),
        ((0, 2, 0), (0, 2, 1)),
        ((3, 3, 1), (3, 1, 0), (1, 3, 1), (1, 1, 0)),
        ((2, 3, 0), (2, 1, 1)),
        ((3, 2, 0), (3, 2, 1), (1, 2, 0), (1, 2, 1)),
        ((2, 3, 1), (2, 1, 0)),
        ((2, 2, 0), (2, 2, 1)),
    )


def slot_row(tiles, rows, cols):
    count, slots = tiles.shape[1], NT * CAP
    slot = lax.broadcasted_iota(jnp.int32, (slots, count), 0)
    named = tiles == (slot >> 1)
    earlier = lax.broadcasted_iota(jnp.int32, (count, count), 0) < lax.broadcasted_iota(jnp.int32, (count, count), 1)
    rank = jnp.dot(
        named.astype(jnp.float32).astype(jnp.bfloat16), earlier.astype(jnp.float32).astype(jnp.bfloat16),
        preferred_element_type=jnp.float32,
    )
    taken = named & (rank == (slot & 1).astype(jnp.float32))
    value = (rows * TILE_SIDE + cols + 1).astype(jnp.float32)
    column = jnp.sum(jnp.where(taken, value, 0.0), axis=1, keepdims=True)
    shape = (slots, slots)
    diagonal = lax.broadcasted_iota(jnp.int32, shape, 0) == lax.broadcasted_iota(jnp.int32, shape, 1)
    line = jnp.sum(jnp.where(diagonal, jnp.broadcast_to(column, shape), 0.0), axis=0, keepdims=True)
    return line.astype(jnp.int32) - 1


def screens_kernel(per_chunk, waits, own_ref, vis_ref, coords_ref, tiles_ref, offsets_ref, all_ref, image_ref, table_ref,
                   send_sems, ring_sems, pair_sems, own_sem, plane_out, plane_in, axis_out, axis_in):
    corr, tile = lax.axis_index("corr"), lax.axis_index("tile")
    planes, plane = lax.axis_size("corr"), lax.axis_size("tile")
    me = corr * plane + tile
    core, y, z = tile & 1, (tile >> 1) & 3, tile >> 3

    def chip(who, a, b):
        there_z = (z + who * a + (1 - who) * b) & 3
        there_y = (y + (1 - who) * a + who * b) & 3
        return (there_z * 4 + there_y) * 2 + who

    first_up, first_down = chip(core, 1, 0), chip(core, 3, 0)
    second_up, second_down = chip(core, 0, 1), chip(core, 0, 3)
    pair = (z * 4 + y) * 2 + (1 - core)
    barrier = pltpu.get_barrier_semaphore()

    def in_plane(t):
        return {"tile": (tile + t) & (plane - 1)}

    def along(t):
        return {"corr": (corr + t) & (planes - 1)}

    def greet(t, carry):
        pl.semaphore_signal(barrier, inc=1, device_id=in_plane(t), device_id_type=pl.DeviceIdType.MESH)
        return carry

    lax.fori_loop(1, plane, greet, 0)
    for t in range(1, planes):
        pl.semaphore_signal(barrier, inc=1, device_id=along(t), device_id_type=pl.DeviceIdType.MESH)
    table_ref[pl.ds(me, 1)] = slot_row(tiles_ref[...], offsets_ref[0:1], offsets_ref[1:2])[None]
    pl.semaphore_wait(barrier, plane + planes - 2)

    def plane_copy(t, source):
        return pltpu.make_async_remote_copy(
            src_ref=table_ref.at[source], dst_ref=table_ref.at[source], send_sem=plane_out.at[t], recv_sem=plane_in.at[t],
            device_id=in_plane(t), device_id_type=pl.DeviceIdType.MESH,
        )

    def axis_copy(t, source):
        rows = table_ref.at[pl.ds(source * plane, plane)]
        return pltpu.make_async_remote_copy(
            src_ref=rows, dst_ref=rows, send_sem=axis_out.at[t], recv_sem=axis_in.at[t],
            device_id=along(t), device_id_type=pl.DeviceIdType.MESH,
        )

    def plane_start(t, carry):
        plane_copy(t, me).start()
        return carry

    def plane_wait(t, carry):
        plane_copy(t, corr * plane + ((tile - t) & (plane - 1))).wait()
        return carry

    half = own_ref.shape[0] // 2
    sent = []

    def place(owner, h):
        return all_ref.at[pl.ds(pl.multiple_of(owner * (2 * half) + h * half, half), half)]

    def unit_index(unit):
        return (unit[0] * 4 + unit[1]) * 2 + unit[2]

    def copy_of(unit, target, sem, number):
        a, b, h = unit
        owner = chip(core, a, b)
        source = own_ref.at[pl.ds(h * half, half)] if (a, b) == (0, 0) else place(owner, h)
        return pltpu.make_async_remote_copy(
            src_ref=source, dst_ref=place(owner, h), send_sem=send_sems.at[number], recv_sem=sem,
            device_id={"tile": target}, device_id_type=pl.DeviceIdType.MESH,
        )

    def push(unit, target, arrives):
        sem = pair_sems.at[unit_index(unit)] if arrives is None else ring_sems.at[unit_index(arrives)]
        copy_of(unit, target, sem, len(sent)).start()
        sent.append(unit)

    def await_ring(unit):
        copy_of(unit, first_up, ring_sems.at[unit_index(unit)], 0).wait_recv()

    def await_pair(unit):
        a, b, h = unit
        owner = chip(1 - core, a, b)
        pltpu.make_async_remote_copy(
            src_ref=place(owner, h), dst_ref=place(owner, h), send_sem=send_sems.at[0],
            recv_sem=pair_sems.at[unit_index(unit)], device_id={"tile": pair}, device_id_type=pl.DeviceIdType.MESH,
        ).wait_recv()

    def forward(unit):
        a, b, h = unit
        if b == 0:
            if (a, h) == (3, 0):
                push(unit, first_up, (2, 0, 0))
            if (a, h) == (1, 1):
                push(unit, first_down, (2, 0, 1))
            up, down = lambda: push(unit, second_up, (a, 3, h)), lambda: push(unit, second_down, (a, 1, h))
            for go in (up, down) if h == 0 else (down, up):
                go()
        elif (b, h) == (3, 0):
            push(unit, second_up, (a, 2, 0))
        elif (b, h) == (1, 1):
            push(unit, second_down, (a, 2, 1))
        push(unit, pair, None)

    push((0, 0, 0), first_up, (3, 0, 0))
    push((0, 0, 1), first_down, (1, 0, 1))
    push((0, 0, 1), first_up, (3, 0, 1))
    push((0, 0, 0), first_down, (1, 0, 0))
    push((0, 0, 0), second_up, (0, 3, 0))
    push((0, 0, 1), second_down, (0, 1, 1))
    push((0, 0, 1), second_up, (0, 3, 1))
    push((0, 0, 0), second_down, (0, 1, 0))
    for h in range(2):
        push((0, 0, h), pair, None)
    local = pltpu.make_async_copy(own_ref, all_ref.at[pl.ds(pl.multiple_of(tile * (2 * half), half), 2 * half)], own_sem)
    local.start()

    first, second = direction_tables()

    def compute(begin, end):
        def step(s, carry):
            u, v, w = (coords_ref[axis, pl.ds(s, 1)] for axis in range(3))
            image_re, image_im = image_of(u, v, w, vis_ref[s], first, second)
            image_ref[s, 0:SUB] = image_re
            image_ref[s, SUB:2 * SUB] = image_im
            return carry

        lax.fori_loop(begin, end, step, 0)

    groups = ring_plan()
    count = vis_ref.shape[0]
    chunks = count // per_chunk

    def chunk(i, carry):
        compute(i * per_chunk, (i + 1) * per_chunk)

        @pl.when(i == 0)
        def _():
            lax.fori_loop(1, plane, plane_start, 0)

        @pl.when(i == chunks - 4)
        def _():
            lax.fori_loop(1, plane, plane_wait, 0)
            for t in range(1, planes):
                axis_copy(t, corr).start()

        for group, when in zip(groups, waits):
            if when is not None:
                @pl.when(i == when)
                def _():
                    for unit in group:
                        await_ring(unit)
                        forward(unit)
        return carry

    lax.fori_loop(0, chunks, chunk, 0)
    for group, when in zip(groups, waits):
        if when is None:
            for unit in group:
                await_ring(unit)
                forward(unit)
    for a in range(4):
        for b in range(4):
            for h in range(2):
                await_pair((a, b, h))
    for number, unit in enumerate(sent):
        copy_of(unit, pair, pair_sems.at[0], number).wait_send()
    for t in range(1, planes):
        axis_copy(t, (corr - t) & (planes - 1)).wait()
    local.wait()


WAITS = (3, 4, 5, 6, 7, 9, 11, 13, None, None, None, None)


def gather_screens(own, visibilities, coords, tiles, offsets, devices, tile_size):
    count = visibilities.shape[0]
    vmem = pl.BlockSpec(memory_space=pltpu.VMEM)
    own_count = own.shape[0]
    copies = 62
    return pl.pallas_call(
        functools.partial(screens_kernel, 4, WAITS),
        out_shape=(
            jax.ShapeDtypeStruct((own_count * tile_size,) + own.shape[1:], own.dtype),
            jax.ShapeDtypeStruct((count, 2 * SUB, LANES), jnp.float32),
            jax.ShapeDtypeStruct((devices, 1, NT * CAP), jnp.int32),
        ),
        in_specs=[vmem] * 5,
        out_specs=(pl.BlockSpec(memory_space=pl.ANY), vmem, vmem),
        scratch_shapes=[
            pltpu.SemaphoreType.DMA((copies,)),
            pltpu.SemaphoreType.DMA((32,)),
            pltpu.SemaphoreType.DMA((32,)),
            pltpu.SemaphoreType.DMA,
            pltpu.SemaphoreType.DMA((tile_size,)),
            pltpu.SemaphoreType.DMA((tile_size,)),
            pltpu.SemaphoreType.DMA((devices // tile_size,)),
            pltpu.SemaphoreType.DMA((devices // tile_size,)),
        ],
        compiler_params=pltpu.CompilerParams(vmem_limit_bytes=VMEM_LIMIT, collective_id=0, has_side_effects=True),
        name="screens",
    )(own, visibilities, coords, tiles, offsets)


def sandwich_of(image, near, far):
    def row(array, index):
        return array[index * NJ:(index + 1) * NJ]

    mid_re, mid_im = {}, {}
    for out_row in range(2):
        for inner in range(2):
            total_re = total_im = None
            for first in range(2):
                n_re, n_im = row(near, 2 * first + out_row), row(near, 4 + 2 * first + out_row)
                v_re, v_im = row(image, 2 * first + inner), row(image, 4 + 2 * first + inner)
                re = n_re * v_re + n_im * v_im
                im = n_re * v_im - n_im * v_re
                total_re = re if total_re is None else total_re + re
                total_im = im if total_im is None else total_im + im
            mid_re[out_row, inner], mid_im[out_row, inner] = total_re, total_im
    out_re, out_im = [], []
    for out_row in range(2):
        for out_col in range(2):
            total_re = total_im = None
            for inner in range(2):
                m_re, m_im = mid_re[out_row, inner], mid_im[out_row, inner]
                f_re, f_im = row(far, 2 * inner + out_col), row(far, 4 + 2 * inner + out_col)
                re = m_re * f_re - m_im * f_im
                im = m_re * f_im + m_im * f_re
                total_re = re if total_re is None else total_re + re
                total_im = im if total_im is None else total_im + im
            out_re.append(total_re)
            out_im.append(total_im)
    return out_re, out_im


def fft8(re, im):
    def add(x, y):
        return x[0] + y[0], x[1] + y[1]

    def sub(x, y):
        return x[0] - y[0], x[1] - y[1]

    def turn(x):
        return x[1], -x[0]

    def fft4(x):
        even_add, even_sub = add(x[0], x[2]), sub(x[0], x[2])
        odd_add, odd_sub = add(x[1], x[3]), turn(sub(x[1], x[3]))
        return [add(even_add, odd_add), add(even_sub, odd_sub), sub(even_add, odd_add), sub(even_sub, odd_sub)]

    x = list(zip(re, im))
    even, odd = fft4(x[0::2]), fft4(x[1::2])
    odd = [
        odd[0],
        ((odd[1][0] + odd[1][1]) * ROOT_HALF, (odd[1][1] - odd[1][0]) * ROOT_HALF),
        turn(odd[2]),
        ((odd[3][1] - odd[3][0]) * ROOT_HALF, (-odd[3][0] - odd[3][1]) * ROOT_HALF),
    ]
    out = [add(even[k], odd[k]) for k in range(4)] + [sub(even[k], odd[k]) for k in range(4)]
    return [(-o[0], -o[1]) if k % 2 else o for k, o in enumerate(out)]


def blocks_kernel(count, stations, tile_ids, image_ref, taper_ref, table_ref, screens, send_ref, near_far, x_re,
                  x_im, y_ref, u_re, u_im, used, sems):
    def fetch(s, which):
        return pltpu.make_async_copy(screens.at[stations[which, s]], near_far.at[s, which], sems.at[s, which])

    def start(s, carry):
        fetch(s, 0).start()
        fetch(s, 1).start()
        return carry

    lax.fori_loop(0, count, start, 0)

    def clear(i, carry):
        used[i] = 0
        return carry

    lax.fori_loop(0, NT, clear, 0)

    taper = taper_ref[...]

    def sandwich(s, carry):
        fetch(s, 0).wait()
        fetch(s, 1).wait()
        near = near_far[s, 0].astype(jnp.float32)
        far = near_far[s, 1].astype(jnp.float32)
        out_re, out_im = sandwich_of(image_ref[s], near, far)
        for e in range(NCORR):
            rows = pl.ds(pl.multiple_of(s * SUB + e * NJ, NJ), NJ)
            x_re[rows] = out_re[e] * taper
            x_im[rows] = out_im[e] * taper
        return carry

    lax.fori_loop(0, count, sandwich, 0, unroll=2)

    chunk = 16

    def transform(i, carry):
        base = i * (chunk * NJ)
        re = [x_re[pl.ds(base + j, chunk, stride=NJ)] for j in range(NJ)]
        im = [x_im[pl.ds(base + j, chunk, stride=NJ)] for j in range(NJ)]
        rows = pl.ds(pl.multiple_of(i * chunk, chunk), chunk)
        for a8, (y_re, y_im) in enumerate(fft8(re, im)):
            y_ref[a8, rows, 0:LANES] = y_re.astype(jnp.bfloat16)
            y_ref[a8, rows, LANES:2 * LANES] = y_im.astype(jnp.bfloat16)
        return carry

    lax.fori_loop(0, count * NCORR // chunk, transform, 0)

    for a8 in range(NJ):
        out = jnp.dot(y_ref[a8], table_ref[a8], preferred_element_type=jnp.float32)
        u_re[pl.ds(a8, count * NCORR, stride=NJ)] = out[:, 0:LANES]
        u_im[pl.ds(a8, count * NCORR, stride=NJ)] = out[:, LANES:2 * LANES]

    def pack(s, carry):
        tile = tile_ids[s]
        rank = used[tile]
        used[tile] = rank + 1
        slot = tile * CAP + rank
        target = pl.ds(pl.multiple_of(slot * 2 * NJ, 2 * NJ), 2 * NJ)
        for e in range(NCORR):
            rows = pl.ds(pl.multiple_of(s * SUB + e * NJ, NJ), NJ)
            send_ref[e, target] = jnp.concatenate([u_re[rows], u_im[rows]], axis=0).astype(jnp.bfloat16)
        return carry

    lax.fori_loop(0, count, pack, 0, unroll=2)


def blocks(image, screens, stations, tile_ids):
    count = image.shape[0]
    vmem = pl.BlockSpec(memory_space=pltpu.VMEM)
    smem = pl.BlockSpec(memory_space=pltpu.SMEM)
    slots = NT * CAP
    points = count * NCORR
    return pl.pallas_call(
        functools.partial(blocks_kernel, count),
        out_shape=jax.ShapeDtypeStruct((NCORR, slots * 2 * NJ, LANES), jnp.bfloat16),
        in_specs=[smem, smem, vmem, vmem, vmem, pl.BlockSpec(memory_space=pl.ANY)],
        out_specs=vmem,
        scratch_shapes=[
            pltpu.VMEM((count, 2, 2 * SUB, LANES), jnp.bfloat16),
            pltpu.VMEM((points * NJ, LANES), jnp.float32),
            pltpu.VMEM((points * NJ, LANES), jnp.float32),
            pltpu.VMEM((NJ, points, 2 * LANES), jnp.bfloat16),
            pltpu.VMEM((points * NJ, LANES), jnp.float32),
            pltpu.VMEM((points * NJ, LANES), jnp.float32),
            pltpu.SMEM((NT,), jnp.int32),
            pltpu.SemaphoreType.DMA((count, 2)),
        ],
        compiler_params=pltpu.CompilerParams(vmem_limit_bytes=VMEM_LIMIT),
        name="blocks",
    )(stations, tile_ids, image, taper_table(), uv_tables(), screens)


def exchange_kernel(per_owner, table, send_ref, out_ref, recv, moved, acc, data_out, data_in, own_sem):
    corr, tile = lax.axis_index("corr"), lax.axis_index("tile")
    planes, plane = lax.axis_size("corr"), lax.axis_size("tile")
    devices = planes * plane
    core, y, z = tile & 1, (tile >> 1) & 3, tile >> 3
    slots = per_owner * CAP

    def there(k, sign):
        d = (k * ORDER) & (devices - 1)
        x1 = (corr + sign * (d >> 5)) & 3
        z1 = (z + sign * (d >> 3)) & 3
        y1 = (y + sign * (d >> 1)) & 3
        return x1, z1 * 8 + y1 * 2 + ((core + d) & 1)

    barrier = pltpu.get_barrier_semaphore()

    def greet(k, carry):
        x1, t1 = there(k, -1)
        pl.semaphore_signal(barrier, inc=1, device_id={"corr": x1, "tile": t1}, device_id_type=pl.DeviceIdType.MESH)
        return carry

    lax.fori_loop(1, devices, greet, 0)
    own = pltpu.make_async_copy(send_ref.at[corr * plane + tile], recv.at[0], own_sem)
    own.start()
    acc[...] = jnp.zeros_like(acc)
    pl.semaphore_wait(barrier, devices - 1)

    def copy_of(k):
        x1, t1 = there(k, 1)
        return pltpu.make_async_remote_copy(
            src_ref=send_ref.at[x1 * plane + t1], dst_ref=recv.at[k], send_sem=data_out.at[k], recv_sem=data_in.at[k],
            device_id={"corr": x1, "tile": t1}, device_id_type=pl.DeviceIdType.MESH,
        )

    def start(k, carry):
        copy_of(k).start()
        return carry

    lax.fori_loop(1, devices, start, 0)
    own.wait()

    lane = lax.broadcasted_iota(jnp.int32, (NJ, LANES), 1)
    batch = 4
    depth = batch * CAP * SUB
    target_lane = lax.broadcasted_iota(jnp.int32, (1, depth), 1)
    target_row = lax.broadcasted_iota(jnp.int32, (TILE_SIDE, depth), 0)

    def group(g, carry):
        firsts = [jnp.zeros((1, depth), jnp.int32) for _ in range(per_owner)]
        for i in range(batch):
            k = g * batch + i

            @pl.when(k > 0)
            def _():
                copy_of(k).wait()

            x1, t1 = there(k, -1)
            source = x1 * plane + t1
            for slot in range(slots):
                place = table[source, tile * slots + slot]
                row0, col0 = place >> 7, place & (TILE_SIDE - 1)
                begin = jnp.where(place >= 0, row0, 2 * LANES)
                inside = (lane >= begin) & (lane < begin + SUB)
                block = recv[k, slot * 2 * NJ:(slot + 1) * 2 * NJ].astype(jnp.float32)
                number = i * CAP + slot % CAP
                for part in range(2):
                    data = block[part * NJ:(part + 1) * NJ]
                    rolled = []
                    for a4 in range(4):
                        shift = (row0 + (LANES - a4 * SUB)) & (LANES - 1)
                        rolled.append(jnp.where(inside, pltpu.roll(data, shift, 1), 0.0))
                    rolled = jnp.concatenate(rolled, axis=0).astype(jnp.bfloat16)
                    moved[slot // CAP, number * SUB:(number + 1) * SUB, part * LANES:(part + 1) * LANES] = rolled
                firsts[slot // CAP] = jnp.where(target_lane >= number * SUB, col0 - number * SUB, firsts[slot // CAP])
        for own_tile in range(per_owner):
            select = (target_row == firsts[own_tile] + target_lane).astype(jnp.float32).astype(jnp.bfloat16)
            acc[own_tile] += jnp.dot(select, moved[own_tile], preferred_element_type=jnp.float32)
        return carry

    lax.fori_loop(0, devices // batch, group, 0)
    for own_tile in range(per_owner):
        for part in range(2):
            out_ref[own_tile, part] = acc[own_tile, :, part * LANES:(part + 1) * LANES].T


ORDER = 37


def exchange(sending, table, per_owner):
    devices = sending.shape[0]
    sems = pltpu.SemaphoreType.DMA((devices,))
    return pl.pallas_call(
        functools.partial(exchange_kernel, per_owner),
        out_shape=jax.ShapeDtypeStruct((per_owner, 2, TILE_SIDE, TILE_SIDE), jnp.float32),
        in_specs=[pl.BlockSpec(memory_space=pltpu.SMEM), pl.BlockSpec(memory_space=pl.ANY)],
        out_specs=pl.BlockSpec(memory_space=pltpu.VMEM),
        scratch_shapes=[
            pltpu.VMEM(sending.shape, sending.dtype),
            pltpu.VMEM((per_owner, 4 * CAP * SUB, 2 * LANES), jnp.bfloat16),
            pltpu.VMEM((per_owner, TILE_SIDE, 2 * LANES), jnp.float32),
            sems,
            sems,
            pltpu.SemaphoreType.DMA,
        ],
        compiler_params=pltpu.CompilerParams(vmem_limit_bytes=VMEM_LIMIT, collective_id=1, has_side_effects=True),
        name="exchange",
    )(table, sending)


def per_device(visibilities, coords, stations, tile_ids, offsets, screens):
    tile_size = lax.axis_size("tile")
    devices = lax.axis_size("corr") * tile_size
    per_owner = NT // tile_size
    own = screens.reshape(screens.shape[0], 2 * SUB, LANES)
    all_screens, image, table = gather_screens(
        own, visibilities, coords.transpose(1, 0, 2), tile_ids.T, offsets.T, devices, tile_size
    )
    sending = blocks(image, all_screens, stations.T, tile_ids[:, 0])
    sending = sending.reshape(devices, per_owner * CAP * 2 * NJ, LANES)
    return exchange(sending, table.reshape(devices, NT * CAP), per_owner)[None]


def solution(mesh):
    return jax.shard_map(
        per_device,
        mesh=mesh,
        in_specs=(
            P(("corr", "tile"), None, None),
            P(("corr", "tile"), None, None),
            P(("corr", "tile"), None),
            P(("corr", "tile"), None),
            P(("corr", "tile"), None),
            P("tile", None, None),
        ),
        out_specs=P("corr", "tile", None, None, None),
        check_vma=False,
    )
```

```python
import functools
import math

import jax
import jax.numpy as jnp
import numpy as np
from jax import lax
from jax.experimental import pallas as pl
from jax.experimental.pallas import tpu as pltpu
from jax.sharding import PartitionSpec as P

SUB = 32
NT = 64
TILE_SIDE = 128
NVIS = 256
PIX = 1024
NCORR = 4
CAP = 2
NJ = 8
LANES = 128
SIN_POLY = (3.141592579805584, -5.167706866167941, 2.550031193519298, -0.5980441939119835, 0.07721838615698538)
COS_POLY = (0.9999999532476082, -4.934792830619647, 4.058411352862557, -1.3318765680805114, 0.2196896110968953)
ROOT_HALF = math.sqrt(0.5)
VMEM_LIMIT = 60 * 1024 * 1024


def uv_tables():
    rr = np.arange(4)[:, None, None, None]
    c = np.arange(SUB)[None, :, None, None]
    a4 = np.arange(4)[None, None, :, None]
    d = np.arange(SUB)[None, None, None, :]
    half = SUB // 2
    tables = []
    for a8 in range(NJ):
        turns = (rr * (a8 + 8 * a4 - half) + (c - half) * (d - half)) % SUB
        angle = (-2.0 * np.pi / SUB) * turns.reshape(LANES, LANES)
        re, im = np.cos(angle) / SUB, np.sin(angle) / SUB
        tables.append(np.block([[re, im], [-im, re]]))
    return jnp.asarray(np.stack(tables), jnp.bfloat16)


def taper_table():
    pos = (np.arange(SUB) - SUB // 2 + 0.5) / (SUB // 2)
    edge = 1.0 - 0.8 * pos * pos
    return jnp.asarray((edge[:, None] * edge[None, :] / NVIS).reshape(NJ, LANES), jnp.float32)


def poly(square, coefficients):
    total = jnp.full_like(square, coefficients[-1])
    for coefficient in coefficients[-2::-1]:
        total = total * square + coefficient
    return total


def cos_sin_turns(turns):
    rest = turns - jnp.round(turns)
    square = rest * rest
    sine = rest * poly(square, SIN_POLY)
    cosine = poly(square, COS_POLY)
    twice = sine + sine
    return 1.0 - twice * sine, twice * cosine


def direction_tables():
    row = lax.broadcasted_iota(jnp.int32, (2 * SUB, NVIS), 0)
    r = (row % NJ) * 4 + row // NJ
    place = jnp.where(row < SUB, r, row - SUB)
    first = (place - SUB // 2).astype(jnp.float32) * (1.0 / SUB)
    return first, -0.5 * first * first


def image_of(u, v, w, vis, first, second):
    linear = jnp.concatenate([u * first[:SUB], v * first[SUB:]], axis=0)
    cosine, sine = cos_sin_turns(linear + w * second)
    row_re, row_im = cosine[:SUB], sine[:SUB]
    col_re, col_im = cosine[SUB:], sine[SUB:]
    vis = vis.astype(jnp.float32)
    lhs = []
    for rr in range(4):
        a_re, a_im = row_re[rr * NJ:(rr + 1) * NJ], row_im[rr * NJ:(rr + 1) * NJ]
        part_re, part_im = [], []
        for e in range(NCORR):
            v_re, v_im = vis[e:e + 1], vis[NCORR + e:NCORR + e + 1]
            part_re.append(v_re * a_re - v_im * a_im)
            part_im.append(v_re * a_im + v_im * a_re)
        lhs.append(jnp.concatenate([jnp.concatenate(part_re, axis=0), jnp.concatenate(part_im, axis=0)], axis=1))
    lhs = jnp.concatenate(lhs, axis=0).astype(jnp.bfloat16)
    upper = jnp.concatenate([col_re, -col_im], axis=1)
    lower = jnp.concatenate([col_im, col_re], axis=1)
    rhs = jnp.concatenate([upper, lower, upper, lower], axis=0).astype(jnp.bfloat16)
    out = lax.dot_general(lhs, rhs, (((1,), (1,)), ((), ())), preferred_element_type=jnp.float32)
    parts = [out[rr * SUB:(rr + 1) * SUB] for rr in range(4)]
    turned = [pltpu.roll(part, SUB, 1) for part in parts]
    lane = lax.broadcasted_iota(jnp.int32, (SUB, LANES), 1)

    def join(a, b, c, d):
        return jnp.where(lane < SUB, a, jnp.where(lane < 2 * SUB, b, jnp.where(lane < 3 * SUB, c, d)))

    image_re = join(parts[0], turned[1], parts[2], turned[3])
    image_im = join(turned[0], parts[1], turned[2], parts[3])
    return image_re, image_im


def ring_plan():
    return (
        ((3, 0, 0), (1, 0, 1)),
        ((3, 0, 1), (1, 0, 0)),
        ((0, 3, 0), (0, 1, 1)),
        ((0, 3, 1), (0, 1, 0)),
        ((2, 0, 0), (2, 0, 1)),
        ((3, 3, 0), (3, 1, 1), (1, 3, 0), (1, 1, 1)),
        ((0, 2, 0), (0, 2, 1)),
        ((3, 3, 1), (3, 1, 0), (1, 3, 1), (1, 1, 0)),
        ((2, 3, 0), (2, 1, 1)),
        ((3, 2, 0), (3, 2, 1), (1, 2, 0), (1, 2, 1)),
        ((2, 3, 1), (2, 1, 0)),
        ((2, 2, 0), (2, 2, 1)),
    )


def sandwich_of(image, near, far):
    def row(array, index):
        return array[index * NJ:(index + 1) * NJ]

    mid_re, mid_im = {}, {}
    for out_row in range(2):
        for inner in range(2):
            total_re = total_im = None
            for first in range(2):
                n_re, n_im = row(near, 2 * first + out_row), row(near, 4 + 2 * first + out_row)
                v_re, v_im = row(image, 2 * first + inner), row(image, 4 + 2 * first + inner)
                re = n_re * v_re + n_im * v_im
                im = n_re * v_im - n_im * v_re
                total_re = re if total_re is None else total_re + re
                total_im = im if total_im is None else total_im + im
            mid_re[out_row, inner], mid_im[out_row, inner] = total_re, total_im
    out_re, out_im = [], []
    for out_row in range(2):
        for out_col in range(2):
            total_re = total_im = None
            for inner in range(2):
                m_re, m_im = mid_re[out_row, inner], mid_im[out_row, inner]
                f_re, f_im = row(far, 2 * inner + out_col), row(far, 4 + 2 * inner + out_col)
                re = m_re * f_re - m_im * f_im
                im = m_re * f_im + m_im * f_re
                total_re = re if total_re is None else total_re + re
                total_im = im if total_im is None else total_im + im
            out_re.append(total_re)
            out_im.append(total_im)
    return out_re, out_im


def fft8(re, im):
    def add(x, y):
        return x[0] + y[0], x[1] + y[1]

    def sub(x, y):
        return x[0] - y[0], x[1] - y[1]

    def turn(x):
        return x[1], -x[0]

    def fft4(x):
        even_add, even_sub = add(x[0], x[2]), sub(x[0], x[2])
        odd_add, odd_sub = add(x[1], x[3]), turn(sub(x[1], x[3]))
        return [add(even_add, odd_add), add(even_sub, odd_sub), sub(even_add, odd_add), sub(even_sub, odd_sub)]

    x = list(zip(re, im))
    even, odd = fft4(x[0::2]), fft4(x[1::2])
    odd = [
        odd[0],
        ((odd[1][0] + odd[1][1]) * ROOT_HALF, (odd[1][1] - odd[1][0]) * ROOT_HALF),
        turn(odd[2]),
        ((odd[3][1] - odd[3][0]) * ROOT_HALF, (-odd[3][0] - odd[3][1]) * ROOT_HALF),
    ]
    out = [add(even[k], odd[k]) for k in range(4)] + [sub(even[k], odd[k]) for k in range(4)]
    return [(-o[0], -o[1]) if k % 2 else o for k, o in enumerate(out)]


def one_hot(mask):
    return mask.astype(jnp.float32).astype(jnp.bfloat16)


def diagonal(n):
    return lax.broadcasted_iota(jnp.int32, (n, n), 0) == lax.broadcasted_iota(jnp.int32, (n, n), 1)


def as_line(column):
    n = column.shape[0]
    return jnp.sum(jnp.where(diagonal(n), jnp.broadcast_to(column, (n, n)), 0), axis=0, keepdims=True)


def slot_lines(tiles, rows, cols):
    count, slots = tiles.shape[1], NT * CAP
    shape = (count, count)
    wide = jnp.broadcast_to(tiles, shape)
    column = jnp.sum(jnp.where(diagonal(count), wide, 0), axis=1, keepdims=True)
    earlier = lax.broadcasted_iota(jnp.int32, shape, 0) < lax.broadcasted_iota(jnp.int32, shape, 1)
    rank = jnp.sum(jnp.where(earlier & (column == wide), 1, 0), axis=0, keepdims=True)
    slot = lax.broadcasted_iota(jnp.int32, (slots, count), 0)
    taken = tiles * CAP + rank == slot
    number = lax.broadcasted_iota(jnp.int32, (slots, count), 1)

    def total(values):
        return as_line(jnp.sum(jnp.where(taken, values, 0), axis=1, keepdims=True))

    return total(number), total(rows + 1) - 1, total(cols)


def grid_kernel(per_chunk, waits, per_owner, stations, own_ref, vis_ref, coords_ref, tiles_ref, offsets_ref, taper_ref,
                uv_ref, out_ref, shards, meta, image, x_re, x_im, y_ref, u_re, u_im, send, recv, moved, acc, order_row,
                order, places_row, places, send_sems, ring_sems, pair_sems, axis_out, axis_in, data_out, data_in, own_sem):
    corr, tile = lax.axis_index("corr"), lax.axis_index("tile")
    planes, plane = lax.axis_size("corr"), lax.axis_size("tile")
    devices = planes * plane
    core, y, z = tile & 1, (tile >> 1) & 3, tile >> 3
    count = vis_ref.shape[0]
    owned = own_ref.shape[0]
    groups_owned = shards.shape[1] - 1
    half = groups_owned // 2

    def chip(who, a, b):
        there_z = (z + who * a + (1 - who) * b) & 3
        there_y = (y + (1 - who) * a + who * b) & 3
        return (there_z * 4 + there_y) * 2 + who

    first_up, first_down = chip(core, 1, 0), chip(core, 3, 0)
    second_up, second_down = chip(core, 0, 1), chip(core, 0, 3)
    pair = (z * 4 + y) * 2 + (1 - core)
    targets = (first_up, first_down, second_up, second_down, pair)

    def along(t):
        return {"corr": (corr + t) & (planes - 1)}

    barrier = pltpu.get_barrier_semaphore()
    for target in targets:
        pl.semaphore_signal(barrier, inc=1, device_id={"tile": target}, device_id_type=pl.DeviceIdType.MESH)
    for t in range(1, planes):
        pl.semaphore_signal(barrier, inc=1, device_id=along(t), device_id_type=pl.DeviceIdType.MESH)

    for i in range(owned):
        screen = own_ref[i].astype(jnp.float32)
        for j in range(NJ):
            x_re[pl.ds(i * 2 * SUB + j, NJ, stride=NJ)] = screen[:, j * LANES:(j + 1) * LANES]
    for i in range(owned):
        screen = x_re[i * 2 * SUB:(i + 1) * 2 * SUB].astype(jnp.bfloat16)
        shards[tile, i * PARTS:(i + 1) * PARTS] = screen.reshape(PARTS, META, LANES)
    number_line, row_line, col_line = slot_lines(tiles_ref[...], offsets_ref[0:1], offsets_ref[1:2])
    kind = lax.broadcasted_iota(jnp.int32, (META, LANES), 0)
    lines = jnp.where(kind == 0, row_line, jnp.where(kind == 1, col_line, 0))
    shards[tile, groups_owned] = lines.astype(jnp.float32).astype(jnp.bfloat16)
    order_row[...] = number_line
    pl.semaphore_wait(barrier, len(targets) + planes - 1)

    sent = []

    def place(owner, h):
        return shards.at[owner, pl.ds(h * half, half + h)]

    def unit_index(unit):
        return (unit[0] * 4 + unit[1]) * 2 + unit[2]

    def unit_copy(owner, h, target, send_sem, sem):
        return pltpu.make_async_remote_copy(
            src_ref=place(owner, h), dst_ref=place(owner, h), send_sem=send_sem, recv_sem=sem,
            device_id={"tile": target}, device_id_type=pl.DeviceIdType.MESH,
        )

    def push(unit, target, arrives):
        sem = pair_sems.at[unit_index(unit)] if arrives is None else ring_sems.at[unit_index(arrives)]
        unit_copy(chip(core, unit[0], unit[1]), unit[2], target, send_sems.at[len(sent)], sem).start()
        sent.append(unit)

    def await_ring(unit):
        owner = chip(core, unit[0], unit[1])
        unit_copy(owner, unit[2], pair, send_sems.at[0], ring_sems.at[unit_index(unit)]).wait_recv()

    def await_pair(unit):
        owner = chip(1 - core, unit[0], unit[1])
        unit_copy(owner, unit[2], pair, send_sems.at[0], pair_sems.at[unit_index(unit)]).wait_recv()

    def forward(unit):
        a, b, h = unit
        if b == 0:
            if (a, h) == (3, 0):
                push(unit, first_up, (2, 0, 0))
            if (a, h) == (1, 1):
                push(unit, first_down, (2, 0, 1))
            up, down = (second_up, (a, 3, h)), (second_down, (a, 1, h))
            for target, arrives in (up, down) if h == 0 else (down, up):
                push(unit, target, arrives)
        elif (b, h) == (3, 0):
            push(unit, second_up, (a, 2, 0))
        elif (b, h) == (1, 1):
            push(unit, second_down, (a, 2, 1))
        push(unit, pair, None)

    push((0, 0, 0), first_up, (3, 0, 0))
    push((0, 0, 1), first_down, (1, 0, 1))
    push((0, 0, 1), first_up, (3, 0, 1))
    push((0, 0, 0), first_down, (1, 0, 0))
    push((0, 0, 0), second_up, (0, 3, 0))
    push((0, 0, 1), second_down, (0, 1, 1))
    push((0, 0, 1), second_up, (0, 3, 1))
    push((0, 0, 0), second_down, (0, 1, 0))
    for h in range(2):
        push((0, 0, h), pair, None)

    first, second = direction_tables()

    def compute(begin, end):
        def step(s, carry):
            u, v, w = (coords_ref[axis, pl.ds(s, 1)] for axis in range(3))
            image_re, image_im = image_of(u, v, w, vis_ref[s], first, second)
            image[s, 0:SUB] = image_re
            image[s, SUB:2 * SUB] = image_im
            return carry

        lax.fori_loop(begin, end, step, 0)

    groups = ring_plan()
    chunks = count // per_chunk

    def chunk(i, carry):
        compute(i * per_chunk, (i + 1) * per_chunk)
        for group, when in zip(groups, waits):
            if when is not None:
                @pl.when(i == when)
                def _():
                    for unit in group:
                        await_ring(unit)
                        forward(unit)
        return carry

    lax.fori_loop(0, chunks, chunk, 0)
    scalars = pltpu.make_async_copy(order_row, order, own_sem)
    scalars.start()
    for group, when in zip(groups, waits):
        if when is None:
            for unit in group:
                await_ring(unit)
                forward(unit)
    for a in range(4):
        for b in range(4):
            for h in range(2):
                await_pair((a, b, h))

    def axis_copy(t, whose):
        return pltpu.make_async_remote_copy(
            src_ref=shards.at[:, groups_owned], dst_ref=meta.at[whose],
            send_sem=axis_out.at[t], recv_sem=axis_in.at[t], device_id=along(t), device_id_type=pl.DeviceIdType.MESH,
        )

    for t in range(1, planes):
        axis_copy(t, corr).start()
    meta[corr] = shards[:, groups_owned]

    taper = taper_ref[...]

    def screen_of(station):
        screen = shards[station >> 4, pl.ds((station & (owned - 1)) * PARTS, PARTS)]
        return screen.reshape(2 * SUB, LANES).astype(jnp.float32)

    def sandwich(s, carry):
        out_re, out_im = sandwich_of(image[s], screen_of(stations[0, s]), screen_of(stations[1, s]))
        for e in range(NCORR):
            rows = pl.ds(pl.multiple_of(s * SUB + e * NJ, NJ), NJ)
            x_re[rows] = out_re[e] * taper
            x_im[rows] = out_im[e] * taper
        return carry

    lax.fori_loop(0, count, sandwich, 0, unroll=2)
    points = 16

    def transform(i, carry):
        base = i * (points * NJ)
        re = [x_re[pl.ds(base + j, points, stride=NJ)] for j in range(NJ)]
        im = [x_im[pl.ds(base + j, points, stride=NJ)] for j in range(NJ)]
        rows = pl.ds(pl.multiple_of(i * points, points), points)
        for a8, (y_re, y_im) in enumerate(fft8(re, im)):
            y_ref[a8, rows, 0:LANES] = y_re.astype(jnp.bfloat16)
            y_ref[a8, rows, LANES:2 * LANES] = y_im.astype(jnp.bfloat16)
        return carry

    lax.fori_loop(0, count * NCORR // points, transform, 0)
    for a8 in range(NJ):
        out = jnp.dot(y_ref[a8], uv_ref[a8], preferred_element_type=jnp.float32)
        u_re[pl.ds(a8, count * NCORR, stride=NJ)] = out[:, 0:LANES]
        u_im[pl.ds(a8, count * NCORR, stride=NJ)] = out[:, LANES:2 * LANES]

    slots = per_owner * CAP
    scalars.wait()

    def pack(owner, carry):
        for slot in range(slots):
            s = order[0, owner * slots + slot]
            for e in range(NCORR):
                rows = pl.ds(s * SUB + e * NJ, NJ)
                both = jnp.concatenate([u_re[rows], u_im[rows]], axis=0)
                send[e * plane + owner, slot * 2 * NJ:(slot + 1) * 2 * NJ] = both.astype(jnp.bfloat16)
        return carry

    lax.fori_loop(0, plane, pack, 0)
    for t in range(1, planes):
        axis_copy(t, (corr - t) & (planes - 1)).wait()

    def there(k, sign):
        d = (k * ORDER) & (devices - 1)
        x1 = (corr + sign * (d >> 5)) & 3
        z1 = (z + sign * (d >> 3)) & 3
        y1 = (y + sign * (d >> 1)) & 3
        return x1, z1 * 8 + y1 * 2 + ((core + d) & 1)

    def data_copy(k):
        x1, t1 = there(k, 1)
        return pltpu.make_async_remote_copy(
            src_ref=send.at[x1 * plane + t1], dst_ref=recv.at[k], send_sem=data_out.at[k], recv_sem=data_in.at[k],
            device_id={"corr": x1, "tile": t1}, device_id_type=pl.DeviceIdType.MESH,
        )

    def start(k, carry):
        data_copy(k).start()
        return carry

    lax.fori_loop(1, devices, start, 0)
    recv[0] = send[corr * plane + tile]
    acc[...] = jnp.zeros_like(acc)

    line = lax.broadcasted_iota(jnp.int32, (NJ, LANES), 0)
    chosen = one_hot(lax.broadcasted_iota(jnp.int32, (NJ, LANES), 1) == tile * slots + line)
    shape = (2 * plane, plane * META)
    picked = lax.broadcasted_iota(jnp.int32, shape, 0)
    picked = (picked & (plane - 1)) * META + (picked >> 5) == lax.broadcasted_iota(jnp.int32, shape, 1)
    picked = one_hot(picked)
    for x in range(planes):
        lines = jnp.dot(picked, meta[x].reshape(plane * META, LANES), preferred_element_type=jnp.float32)
        part = lax.dot_general(
            chosen, lines.astype(jnp.bfloat16), (((1,), (1,)), ((), ())), preferred_element_type=jnp.float32
        )
        places_row[x] = jnp.concatenate([part, part], axis=1).astype(jnp.int32)
    scalars = pltpu.make_async_copy(places_row, places, own_sem)
    scalars.start()
    scalars.wait()

    lane = lax.broadcasted_iota(jnp.int32, (NJ, LANES), 1)
    batch = 4
    depth = batch * CAP * SUB
    target_lane = lax.broadcasted_iota(jnp.int32, (1, depth), 1)
    target_row = lax.broadcasted_iota(jnp.int32, (TILE_SIDE, depth), 0)

    def group(g, carry):
        firsts = [jnp.zeros((1, depth), jnp.int32) for _ in range(per_owner)]
        for i in range(batch):
            k = g * batch + i

            @pl.when(k > 0)
            def _():
                data_copy(k).wait()

            x1, t1 = there(k, -1)
            for slot in range(slots):
                row0, col0 = places[x1, slot, t1], places[x1, slot, plane + t1]
                begin = jnp.where(row0 >= 0, row0, 2 * LANES)
                inside = (lane >= begin) & (lane < begin + SUB)
                block = recv[k, slot * 2 * NJ:(slot + 1) * 2 * NJ].astype(jnp.float32)
                number = i * CAP + slot % CAP
                for part in range(2):
                    data = block[part * NJ:(part + 1) * NJ]
                    rolled = []
                    for a4 in range(4):
                        shift = (row0 + (LANES - a4 * SUB)) & (LANES - 1)
                        rolled.append(jnp.where(inside, pltpu.roll(data, shift, 1), 0.0))
                    rolled = jnp.concatenate(rolled, axis=0).astype(jnp.bfloat16)
                    moved[slot // CAP, number * SUB:(number + 1) * SUB, part * LANES:(part + 1) * LANES] = rolled
                firsts[slot // CAP] = jnp.where(target_lane >= number * SUB, col0 - number * SUB, firsts[slot // CAP])
        for own_tile in range(per_owner):
            select = one_hot(target_row == firsts[own_tile] + target_lane)
            acc[own_tile] += jnp.dot(select, moved[own_tile], preferred_element_type=jnp.float32)
        return carry

    lax.fori_loop(0, devices // batch, group, 0)
    for own_tile in range(per_owner):
        for part in range(2):
            out_ref[own_tile, part] = acc[own_tile, :, part * LANES:(part + 1) * LANES].T
    for number, unit in enumerate(sent):
        unit_copy(chip(core, unit[0], unit[1]), unit[2], pair, send_sems.at[number], pair_sems.at[0]).wait_send()


WAITS = (3, 4, 5, 6, 7, 9, 11, 13, None, None, None, None)
ORDER = 37
META = 16
PARTS = 2 * SUB // META


def per_device(visibilities, coords, stations, tile_ids, offsets, screens):
    planes, plane = lax.axis_size("corr"), lax.axis_size("tile")
    devices = planes * plane
    per_owner = NT // plane
    count = visibilities.shape[0]
    points = count * NCORR
    block = (devices, per_owner * CAP * 2 * NJ, LANES)
    vmem = pl.BlockSpec(memory_space=pltpu.VMEM)
    dma = pltpu.SemaphoreType.DMA
    return pl.pallas_call(
        functools.partial(grid_kernel, 4, WAITS, per_owner),
        out_shape=jax.ShapeDtypeStruct((per_owner, 2, TILE_SIDE, TILE_SIDE), jnp.float32),
        in_specs=[pl.BlockSpec(memory_space=pltpu.SMEM)] + [vmem] * 7,
        out_specs=vmem,
        scratch_shapes=[
            pltpu.VMEM((plane, screens.shape[0] * PARTS + 1, META, LANES), jnp.bfloat16),
            pltpu.VMEM((planes, plane, META, LANES), jnp.bfloat16),
            pltpu.VMEM((count, 2 * SUB, LANES), jnp.float32),
            pltpu.VMEM((points * NJ, LANES), jnp.float32),
            pltpu.VMEM((points * NJ, LANES), jnp.float32),
            pltpu.VMEM((NJ, points, 2 * LANES), jnp.bfloat16),
            pltpu.VMEM((points * NJ, LANES), jnp.float32),
            pltpu.VMEM((points * NJ, LANES), jnp.float32),
            pltpu.VMEM(block, jnp.bfloat16),
            pltpu.VMEM(block, jnp.bfloat16),
            pltpu.VMEM((per_owner, 4 * CAP * SUB, 2 * LANES), jnp.bfloat16),
            pltpu.VMEM((per_owner, TILE_SIDE, 2 * LANES), jnp.float32),
            pltpu.VMEM((1, NT * CAP), jnp.int32),
            pltpu.SMEM((1, NT * CAP), jnp.int32),
            pltpu.VMEM((planes, NJ, LANES), jnp.int32),
            pltpu.SMEM((planes, NJ, LANES), jnp.int32),
            dma((62,)),
            dma((32,)),
            dma((32,)),
            dma((planes,)),
            dma((planes,)),
            dma((devices,)),
            dma((devices,)),
            dma,
        ],
        compiler_params=pltpu.CompilerParams(vmem_limit_bytes=VMEM_LIMIT, collective_id=0, has_side_effects=True),
        name="grid",
    )(stations.T, screens, visibilities, coords.transpose(1, 0, 2), tile_ids.T, offsets.T, taper_table(), uv_tables())[None]


def solution(mesh):
    return jax.shard_map(
        per_device,
        mesh=mesh,
        in_specs=(
            P(("corr", "tile"), None, None),
            P(("corr", "tile"), None, None),
            P(("corr", "tile"), None),
            P(("corr", "tile"), None),
            P(("corr", "tile"), None),
            P("tile", None, None),
        ),
        out_specs=P("corr", "tile", None, None, None),
        check_vma=False,
    )
```

```python
import functools
import math

import jax
import jax.numpy as jnp
import numpy as np
from jax import lax
from jax.experimental import pallas as pl
from jax.experimental.pallas import tpu as pltpu
from jax.sharding import PartitionSpec as P

SUB = 32
NT = 64
TILE_SIDE = 128
NVIS = 256
PIX = 1024
NCORR = 4
CAP = 2
NJ = 8
LANES = 128
SIN_POLY = (3.141592579805584, -5.167706866167941, 2.550031193519298, -0.5980441939119835, 0.07721838615698538)
COS_POLY = (0.9999999532476082, -4.934792830619647, 4.058411352862557, -1.3318765680805114, 0.2196896110968953)
ROOT_HALF = math.sqrt(0.5)
VMEM_LIMIT = 60 * 1024 * 1024


def uv_tables():
    rr = np.arange(4)[:, None, None, None]
    c = np.arange(SUB)[None, :, None, None]
    a4 = np.arange(4)[None, None, :, None]
    d = np.arange(SUB)[None, None, None, :]
    half = SUB // 2
    tables = []
    for a8 in range(NJ):
        turns = (rr * (a8 + 8 * a4 - half) + (c - half) * (d - half)) % SUB
        angle = (-2.0 * np.pi / SUB) * turns.reshape(LANES, LANES)
        re, im = np.cos(angle) / SUB, np.sin(angle) / SUB
        tables.append(np.block([[re, im], [-im, re]]))
    return jnp.asarray(np.stack(tables), jnp.bfloat16)


def taper_table():
    pos = (np.arange(SUB) - SUB // 2 + 0.5) / (SUB // 2)
    edge = 1.0 - 0.8 * pos * pos
    return jnp.asarray((edge[:, None] * edge[None, :] / NVIS).reshape(NJ, LANES), jnp.float32)


def poly(square, coefficients):
    total = jnp.full_like(square, coefficients[-1])
    for coefficient in coefficients[-2::-1]:
        total = total * square + coefficient
    return total


def cos_sin_turns(turns):
    rest = turns - jnp.round(turns)
    square = rest * rest
    sine = rest * poly(square, SIN_POLY)
    cosine = poly(square, COS_POLY)
    twice = sine + sine
    return 1.0 - twice * sine, twice * cosine


def direction_tables():
    row = lax.broadcasted_iota(jnp.int32, (2 * SUB, NVIS), 0)
    r = (row % NJ) * 4 + row // NJ
    place = jnp.where(row < SUB, r, row - SUB)
    first = (place - SUB // 2).astype(jnp.float32) * (1.0 / SUB)
    return first, -0.5 * first * first


def image_of(u, v, w, vis, first, second):
    linear = jnp.concatenate([u * first[:SUB], v * first[SUB:]], axis=0)
    cosine, sine = cos_sin_turns(linear + w * second)
    row_re, row_im = cosine[:SUB], sine[:SUB]
    col_re, col_im = cosine[SUB:], sine[SUB:]
    vis = vis.astype(jnp.float32)
    lhs = []
    for rr in range(4):
        a_re, a_im = row_re[rr * NJ:(rr + 1) * NJ], row_im[rr * NJ:(rr + 1) * NJ]
        part_re, part_im = [], []
        for e in range(NCORR):
            v_re, v_im = vis[e:e + 1], vis[NCORR + e:NCORR + e + 1]
            part_re.append(v_re * a_re - v_im * a_im)
            part_im.append(v_re * a_im + v_im * a_re)
        lhs.append(jnp.concatenate([jnp.concatenate(part_re, axis=0), jnp.concatenate(part_im, axis=0)], axis=1))
    lhs = jnp.concatenate(lhs, axis=0).astype(jnp.bfloat16)
    upper = jnp.concatenate([col_re, -col_im], axis=1)
    lower = jnp.concatenate([col_im, col_re], axis=1)
    rhs = jnp.concatenate([upper, lower, upper, lower], axis=0).astype(jnp.bfloat16)
    out = lax.dot_general(lhs, rhs, (((1,), (1,)), ((), ())), preferred_element_type=jnp.float32)
    parts = [out[rr * SUB:(rr + 1) * SUB] for rr in range(4)]
    turned = [pltpu.roll(part, SUB, 1) for part in parts]
    lane = lax.broadcasted_iota(jnp.int32, (SUB, LANES), 1)

    def join(a, b, c, d):
        return jnp.where(lane < SUB, a, jnp.where(lane < 2 * SUB, b, jnp.where(lane < 3 * SUB, c, d)))

    image_re = join(parts[0], turned[1], parts[2], turned[3])
    image_im = join(turned[0], parts[1], turned[2], parts[3])
    return image_re, image_im


def ring_plan():
    return (
        ((3, 0, 0), (1, 0, 1)),
        ((3, 0, 1), (1, 0, 0)),
        ((0, 3, 0), (0, 1, 1)),
        ((0, 3, 1), (0, 1, 0)),
        ((2, 0, 0), (2, 0, 1)),
        ((3, 3, 0), (3, 1, 1), (1, 3, 0), (1, 1, 1)),
        ((0, 2, 0), (0, 2, 1)),
        ((3, 3, 1), (3, 1, 0), (1, 3, 1), (1, 1, 0)),
        ((2, 3, 0), (2, 1, 1)),
        ((3, 2, 0), (3, 2, 1), (1, 2, 0), (1, 2, 1)),
        ((2, 3, 1), (2, 1, 0)),
        ((2, 2, 0), (2, 2, 1)),
    )


def sandwich_of(image, near, far):
    def row(array, index):
        return array[index * NJ:(index + 1) * NJ]

    mid_re, mid_im = {}, {}
    for out_row in range(2):
        for inner in range(2):
            total_re = total_im = None
            for first in range(2):
                n_re, n_im = row(near, 2 * first + out_row), row(near, 4 + 2 * first + out_row)
                v_re, v_im = row(image, 2 * first + inner), row(image, 4 + 2 * first + inner)
                re = n_re * v_re + n_im * v_im
                im = n_re * v_im - n_im * v_re
                total_re = re if total_re is None else total_re + re
                total_im = im if total_im is None else total_im + im
            mid_re[out_row, inner], mid_im[out_row, inner] = total_re, total_im
    out_re, out_im = [], []
    for out_row in range(2):
        for out_col in range(2):
            total_re = total_im = None
            for inner in range(2):
                m_re, m_im = mid_re[out_row, inner], mid_im[out_row, inner]
                f_re, f_im = row(far, 2 * inner + out_col), row(far, 4 + 2 * inner + out_col)
                re = m_re * f_re - m_im * f_im
                im = m_re * f_im + m_im * f_re
                total_re = re if total_re is None else total_re + re
                total_im = im if total_im is None else total_im + im
            out_re.append(total_re)
            out_im.append(total_im)
    return out_re, out_im


def fft8(re, im):
    def add(x, y):
        return x[0] + y[0], x[1] + y[1]

    def sub(x, y):
        return x[0] - y[0], x[1] - y[1]

    def turn(x):
        return x[1], -x[0]

    def fft4(x):
        even_add, even_sub = add(x[0], x[2]), sub(x[0], x[2])
        odd_add, odd_sub = add(x[1], x[3]), turn(sub(x[1], x[3]))
        return [add(even_add, odd_add), add(even_sub, odd_sub), sub(even_add, odd_add), sub(even_sub, odd_sub)]

    x = list(zip(re, im))
    even, odd = fft4(x[0::2]), fft4(x[1::2])
    odd = [
        odd[0],
        ((odd[1][0] + odd[1][1]) * ROOT_HALF, (odd[1][1] - odd[1][0]) * ROOT_HALF),
        turn(odd[2]),
        ((odd[3][1] - odd[3][0]) * ROOT_HALF, (-odd[3][0] - odd[3][1]) * ROOT_HALF),
    ]
    out = [add(even[k], odd[k]) for k in range(4)] + [sub(even[k], odd[k]) for k in range(4)]
    return [(-o[0], -o[1]) if k % 2 else o for k, o in enumerate(out)]


def one_hot(mask):
    return mask.astype(jnp.float32).astype(jnp.bfloat16)


def diagonal(n):
    return lax.broadcasted_iota(jnp.int32, (n, n), 0) == lax.broadcasted_iota(jnp.int32, (n, n), 1)


def as_line(column):
    n = column.shape[0]
    return jnp.sum(jnp.where(diagonal(n), jnp.broadcast_to(column, (n, n)), 0), axis=0, keepdims=True)


def slot_lines(tiles, rows, cols):
    count, slots = tiles.shape[1], NT * CAP
    shape = (count, count)
    wide = jnp.broadcast_to(tiles, shape)
    column = jnp.sum(jnp.where(diagonal(count), wide, 0), axis=1, keepdims=True)
    earlier = lax.broadcasted_iota(jnp.int32, shape, 0) < lax.broadcasted_iota(jnp.int32, shape, 1)
    rank = jnp.sum(jnp.where(earlier & (column == wide), 1, 0), axis=0, keepdims=True)
    slot = lax.broadcasted_iota(jnp.int32, (slots, count), 0)
    taken = tiles * CAP + rank == slot
    number = lax.broadcasted_iota(jnp.int32, (slots, count), 1)

    def total(values):
        return as_line(jnp.sum(jnp.where(taken, values, 0), axis=1, keepdims=True))

    return total(number), total(rows + 1) - 1, total(cols)


def grid_kernel(per_chunk, waits, per_owner, stations, own_ref, vis_ref, coords_ref, tiles_ref, offsets_ref, taper_ref,
                uv_ref, out_ref, shards, meta, image, x_re, x_im, y_ref, u_re, u_im, send, recv, moved, acc, order_row,
                order, places_row, places, send_sems, ring_sems, pair_sems, axis_out, axis_in, data_out, data_in, own_sem):
    corr, tile = lax.axis_index("corr"), lax.axis_index("tile")
    planes, plane = lax.axis_size("corr"), lax.axis_size("tile")
    devices = planes * plane
    core, y, z = tile & 1, (tile >> 1) & 3, tile >> 3
    count = vis_ref.shape[0]
    owned = own_ref.shape[0]
    groups_owned = shards.shape[1] - 1
    half = groups_owned // 2

    def chip(who, a, b):
        there_z = (z + who * a + (1 - who) * b) & 3
        there_y = (y + (1 - who) * a + who * b) & 3
        return (there_z * 4 + there_y) * 2 + who

    first_up, first_down = chip(core, 1, 0), chip(core, 3, 0)
    second_up, second_down = chip(core, 0, 1), chip(core, 0, 3)
    pair = (z * 4 + y) * 2 + (1 - core)
    targets = (first_up, first_down, second_up, second_down, pair)

    def along(t):
        return {"corr": (corr + t) & (planes - 1)}

    barrier = pltpu.get_barrier_semaphore()
    for target in targets:
        pl.semaphore_signal(barrier, inc=1, device_id={"tile": target}, device_id_type=pl.DeviceIdType.MESH)
    for t in range(1, planes):
        pl.semaphore_signal(barrier, inc=1, device_id=along(t), device_id_type=pl.DeviceIdType.MESH)

    for i in range(owned):
        screen = own_ref[i].astype(jnp.float32)
        for j in range(NJ):
            x_re[pl.ds(i * 2 * SUB + j, NJ, stride=NJ)] = screen[:, j * LANES:(j + 1) * LANES]
    for i in range(owned):
        screen = x_re[i * 2 * SUB:(i + 1) * 2 * SUB].astype(jnp.bfloat16)
        shards[tile, i * PARTS:(i + 1) * PARTS] = screen.reshape(PARTS, META, LANES)
    number_line, row_line, col_line = slot_lines(tiles_ref[...], offsets_ref[0:1], offsets_ref[1:2])
    kind = lax.broadcasted_iota(jnp.int32, (META, LANES), 0)
    lines = jnp.where(kind == 0, row_line, jnp.where(kind == 1, col_line, 0))
    shards[tile, groups_owned] = lines.astype(jnp.float32).astype(jnp.bfloat16)
    order_row[...] = number_line
    pl.semaphore_wait(barrier, len(targets) + planes - 1)

    sent = []

    def place(owner, h):
        return shards.at[owner, pl.ds(h * half, half + h)]

    def unit_index(unit):
        return (unit[0] * 4 + unit[1]) * 2 + unit[2]

    def unit_copy(owner, h, target, send_sem, sem):
        return pltpu.make_async_remote_copy(
            src_ref=place(owner, h), dst_ref=place(owner, h), send_sem=send_sem, recv_sem=sem,
            device_id={"tile": target}, device_id_type=pl.DeviceIdType.MESH,
        )

    def push(unit, target, arrives):
        sem = pair_sems.at[unit_index(unit)] if arrives is None else ring_sems.at[unit_index(arrives)]
        unit_copy(chip(core, unit[0], unit[1]), unit[2], target, send_sems.at[len(sent)], sem).start()
        sent.append(unit)

    def await_ring(unit):
        owner = chip(core, unit[0], unit[1])
        unit_copy(owner, unit[2], pair, send_sems.at[0], ring_sems.at[unit_index(unit)]).wait_recv()

    def await_pair(unit):
        owner = chip(1 - core, unit[0], unit[1])
        unit_copy(owner, unit[2], pair, send_sems.at[0], pair_sems.at[unit_index(unit)]).wait_recv()

    def forward(unit):
        a, b, h = unit
        if b == 0:
            if (a, h) == (3, 0):
                push(unit, first_up, (2, 0, 0))
            if (a, h) == (1, 1):
                push(unit, first_down, (2, 0, 1))
            up, down = (second_up, (a, 3, h)), (second_down, (a, 1, h))
            for target, arrives in (up, down) if h == 0 else (down, up):
                push(unit, target, arrives)
        elif (b, h) == (3, 0):
            push(unit, second_up, (a, 2, 0))
        elif (b, h) == (1, 1):
            push(unit, second_down, (a, 2, 1))
        push(unit, pair, None)

    push((0, 0, 0), first_up, (3, 0, 0))
    push((0, 0, 1), first_down, (1, 0, 1))
    push((0, 0, 1), first_up, (3, 0, 1))
    push((0, 0, 0), first_down, (1, 0, 0))
    push((0, 0, 0), second_up, (0, 3, 0))
    push((0, 0, 1), second_down, (0, 1, 1))
    push((0, 0, 1), second_up, (0, 3, 1))
    push((0, 0, 0), second_down, (0, 1, 0))
    for h in range(2):
        push((0, 0, h), pair, None)

    first, second = direction_tables()

    def compute(begin):
        def step(s, carry):
            u, v, w = (coords_ref[axis, pl.ds(s, 1)] for axis in range(3))
            image_re, image_im = image_of(u, v, w, vis_ref[s], first, second)
            image[s, 0:SUB] = image_re
            image[s, SUB:2 * SUB] = image_im
            return carry

        for q in range(per_chunk):
            step(begin + q, 0)

    groups = ring_plan()
    chunks = count // per_chunk

    def chunk(i, carry):
        compute(i * per_chunk)
        for group, when in zip(groups, waits):
            if when is not None:
                @pl.when(i == when)
                def _():
                    for unit in group:
                        await_ring(unit)
                        forward(unit)
        return carry

    lax.fori_loop(0, chunks, chunk, 0)
    scalars = pltpu.make_async_copy(order_row, order, own_sem)
    scalars.start()
    for group, when in zip(groups, waits):
        if when is None:
            for unit in group:
                await_ring(unit)
                forward(unit)
    for a in range(4):
        for b in range(4):
            for h in range(2):
                await_pair((a, b, h))

    shape = (2 * plane, plane * META)
    picked = lax.broadcasted_iota(jnp.int32, shape, 0)
    picked = (picked & (plane - 1)) * META + (picked >> 5) == lax.broadcasted_iota(jnp.int32, shape, 1)
    picked = one_hot(picked)
    lines = jnp.dot(picked, shards[:, groups_owned].reshape(plane * META, LANES), preferred_element_type=jnp.float32)
    meta[corr] = lines.astype(jnp.bfloat16)

    def axis_copy(t, whose):
        return pltpu.make_async_remote_copy(
            src_ref=meta.at[whose], dst_ref=meta.at[whose],
            send_sem=axis_out.at[t], recv_sem=axis_in.at[t], device_id=along(t), device_id_type=pl.DeviceIdType.MESH,
        )

    taper = taper_ref[...]

    def screen_of(station):
        screen = shards[station >> 4, pl.ds((station & (owned - 1)) * PARTS, PARTS)]
        return screen.reshape(2 * SUB, LANES).astype(jnp.float32)

    def sandwich(s, carry):
        out_re, out_im = sandwich_of(image[s], screen_of(stations[0, s]), screen_of(stations[1, s]))
        for e in range(NCORR):
            rows = pl.ds(pl.multiple_of(s * SUB + e * NJ, NJ), NJ)
            x_re[rows] = out_re[e] * taper
            x_im[rows] = out_im[e] * taper
        return carry

    lead = count // 8
    lax.fori_loop(0, lead, sandwich, 0, unroll=2)
    for t in range(1, planes):
        axis_copy(t, corr).start()
    lax.fori_loop(lead, count, sandwich, 0, unroll=2)
    points = 16

    def transform(i, carry):
        base = i * (points * NJ)
        re = [x_re[pl.ds(base + j, points, stride=NJ)] for j in range(NJ)]
        im = [x_im[pl.ds(base + j, points, stride=NJ)] for j in range(NJ)]
        rows = pl.ds(pl.multiple_of(i * points, points), points)
        for a8, (y_re, y_im) in enumerate(fft8(re, im)):
            y_ref[a8, rows, 0:LANES] = y_re.astype(jnp.bfloat16)
            y_ref[a8, rows, LANES:2 * LANES] = y_im.astype(jnp.bfloat16)
        return carry

    lax.fori_loop(0, count * NCORR // points, transform, 0)
    for a8 in range(NJ):
        out = jnp.dot(y_ref[a8], uv_ref[a8], preferred_element_type=jnp.float32)
        u_re[pl.ds(a8, count * NCORR, stride=NJ)] = out[:, 0:LANES]
        u_im[pl.ds(a8, count * NCORR, stride=NJ)] = out[:, LANES:2 * LANES]

    slots = per_owner * CAP
    scalars.wait()

    def pack(owner, carry):
        for slot in range(slots):
            s = order[0, owner * slots + slot]
            for e in range(NCORR):
                rows = pl.ds(s * SUB + e * NJ, NJ)
                both = jnp.concatenate([u_re[rows], u_im[rows]], axis=0)
                send[e * plane + owner, slot * 2 * NJ:(slot + 1) * 2 * NJ] = both.astype(jnp.bfloat16)
        return carry

    lax.fori_loop(0, plane, pack, 0)
    for t in range(1, planes):
        axis_copy(t, (corr - t) & (planes - 1)).wait()

    def there(k, sign):
        d = (k * ORDER) & (devices - 1)
        x1 = (corr + sign * (d >> 5)) & 3
        z1 = (z + sign * (d >> 3)) & 3
        y1 = (y + sign * (d >> 1)) & 3
        return x1, z1 * 8 + y1 * 2 + ((core + d) & 1)

    def data_copy(k):
        x1, t1 = there(k, 1)
        return pltpu.make_async_remote_copy(
            src_ref=send.at[x1 * plane + t1], dst_ref=recv.at[k], send_sem=data_out.at[k], recv_sem=data_in.at[k],
            device_id={"corr": x1, "tile": t1}, device_id_type=pl.DeviceIdType.MESH,
        )

    def start(k, carry):
        data_copy(k).start()
        return carry

    recv[0] = send[corr * plane + tile]
    acc[...] = jnp.zeros_like(acc)
    lax.fori_loop(1, devices, start, 0)

    line = lax.broadcasted_iota(jnp.int32, (NJ, LANES), 0)
    chosen = one_hot(lax.broadcasted_iota(jnp.int32, (NJ, LANES), 1) == tile * slots + line)
    for x in range(planes):
        part = lax.dot_general(chosen, meta[x], (((1,), (1,)), ((), ())), preferred_element_type=jnp.float32)
        places_row[x] = jnp.concatenate([part, part], axis=1).astype(jnp.int32)
    scalars = pltpu.make_async_copy(places_row, places, own_sem)
    scalars.start()
    scalars.wait()

    lane = lax.broadcasted_iota(jnp.int32, (NJ, LANES), 1)
    batch = 4
    depth = batch * CAP * SUB
    target_lane = lax.broadcasted_iota(jnp.int32, (1, depth), 1)
    target_row = lax.broadcasted_iota(jnp.int32, (TILE_SIDE, depth), 0)

    def group(g, carry):
        firsts = [jnp.zeros((1, depth), jnp.int32) for _ in range(per_owner)]
        for i in range(batch):
            k = g * batch + i

            @pl.when(k > 0)
            def _():
                data_copy(k).wait()

            x1, t1 = there(k, -1)
            for slot in range(slots):
                row0, col0 = places[x1, slot, t1], places[x1, slot, plane + t1]
                begin = jnp.where(row0 >= 0, row0, 2 * LANES)
                inside = (lane >= begin) & (lane < begin + SUB)
                block = recv[k, slot * 2 * NJ:(slot + 1) * 2 * NJ].astype(jnp.float32)
                number = i * CAP + slot % CAP
                for part in range(2):
                    data = block[part * NJ:(part + 1) * NJ]
                    rolled = []
                    for a4 in range(4):
                        shift = (row0 + (LANES - a4 * SUB)) & (LANES - 1)
                        rolled.append(jnp.where(inside, pltpu.roll(data, shift, 1), 0.0))
                    rolled = jnp.concatenate(rolled, axis=0).astype(jnp.bfloat16)
                    moved[slot // CAP, number * SUB:(number + 1) * SUB, part * LANES:(part + 1) * LANES] = rolled
                firsts[slot // CAP] = jnp.where(target_lane >= number * SUB, col0 - number * SUB, firsts[slot // CAP])
        for own_tile in range(per_owner):
            select = one_hot(target_row == firsts[own_tile] + target_lane)
            acc[own_tile] += jnp.dot(select, moved[own_tile], preferred_element_type=jnp.float32)
        return carry

    lax.fori_loop(0, devices // batch, group, 0)
    for own_tile in range(per_owner):
        for part in range(2):
            out_ref[own_tile, part] = acc[own_tile, :, part * LANES:(part + 1) * LANES].T
    for number, unit in enumerate(sent):
        unit_copy(chip(core, unit[0], unit[1]), unit[2], pair, send_sems.at[number], pair_sems.at[0]).wait_send()


WAITS = (3, 4, 5, 6, 7, 9, 11, 13, None, None, None, None)
ORDER = 37
META = 16
PARTS = 2 * SUB // META


def per_device(visibilities, coords, stations, tile_ids, offsets, screens):
    planes, plane = lax.axis_size("corr"), lax.axis_size("tile")
    devices = planes * plane
    per_owner = NT // plane
    count = visibilities.shape[0]
    points = count * NCORR
    block = (devices, per_owner * CAP * 2 * NJ, LANES)
    vmem = pl.BlockSpec(memory_space=pltpu.VMEM)
    dma = pltpu.SemaphoreType.DMA
    return pl.pallas_call(
        functools.partial(grid_kernel, 4, WAITS, per_owner),
        out_shape=jax.ShapeDtypeStruct((per_owner, 2, TILE_SIDE, TILE_SIDE), jnp.float32),
        in_specs=[pl.BlockSpec(memory_space=pltpu.SMEM)] + [vmem] * 7,
        out_specs=vmem,
        scratch_shapes=[
            pltpu.VMEM((plane, screens.shape[0] * PARTS + 1, META, LANES), jnp.bfloat16),
            pltpu.VMEM((planes, 2 * plane, LANES), jnp.bfloat16),
            pltpu.VMEM((count, 2 * SUB, LANES), jnp.float32),
            pltpu.VMEM((points * NJ, LANES), jnp.float32),
            pltpu.VMEM((points * NJ, LANES), jnp.float32),
            pltpu.VMEM((NJ, points, 2 * LANES), jnp.bfloat16),
            pltpu.VMEM((points * NJ, LANES), jnp.float32),
            pltpu.VMEM((points * NJ, LANES), jnp.float32),
            pltpu.VMEM(block, jnp.bfloat16),
            pltpu.VMEM(block, jnp.bfloat16),
            pltpu.VMEM((per_owner, 4 * CAP * SUB, 2 * LANES), jnp.bfloat16),
            pltpu.VMEM((per_owner, TILE_SIDE, 2 * LANES), jnp.float32),
            pltpu.VMEM((1, NT * CAP), jnp.int32),
            pltpu.SMEM((1, NT * CAP), jnp.int32),
            pltpu.VMEM((planes, NJ, LANES), jnp.int32),
            pltpu.SMEM((planes, NJ, LANES), jnp.int32),
            dma((62,)),
            dma((32,)),
            dma((32,)),
            dma((planes,)),
            dma((planes,)),
            dma((devices,)),
            dma((devices,)),
            dma,
        ],
        compiler_params=pltpu.CompilerParams(vmem_limit_bytes=VMEM_LIMIT, collective_id=0, has_side_effects=True),
        name="grid",
    )(stations.T, screens, visibilities, coords.transpose(1, 0, 2), tile_ids.T, offsets.T, taper_table(), uv_tables())[None]


def solution(mesh):
    return jax.shard_map(
        per_device,
        mesh=mesh,
        in_specs=(
            P(("corr", "tile"), None, None),
            P(("corr", "tile"), None, None),
            P(("corr", "tile"), None),
            P(("corr", "tile"), None),
            P(("corr", "tile"), None),
            P("tile", None, None),
        ),
        out_specs=P("corr", "tile", None, None, None),
        check_vma=False,
    )
```

```python
import functools
import math

import jax
import jax.numpy as jnp
import numpy as np
from jax import lax
from jax.experimental import pallas as pl
from jax.experimental.pallas import tpu as pltpu
from jax.sharding import PartitionSpec as P

SUB = 32
NT = 64
TILE_SIDE = 128
NVIS = 256
PIX = 1024
NCORR = 4
CAP = 2
NJ = 8
LANES = 128
SIN_POLY = (3.141592579805584, -5.167706866167941, 2.550031193519298, -0.5980441939119835, 0.07721838615698538)
COS_POLY = (0.9999999532476082, -4.934792830619647, 4.058411352862557, -1.3318765680805114, 0.2196896110968953)
ROOT_HALF = math.sqrt(0.5)
VMEM_LIMIT = 60 * 1024 * 1024


def uv_tables():
    rr = np.arange(4)[:, None, None, None]
    c = np.arange(SUB)[None, :, None, None]
    a4 = np.arange(4)[None, None, :, None]
    d = np.arange(SUB)[None, None, None, :]
    half = SUB // 2
    tables = []
    for a8 in range(NJ):
        turns = (rr * (a8 + 8 * a4 - half) + (c - half) * (d - half)) % SUB
        angle = (-2.0 * np.pi / SUB) * turns.reshape(LANES, LANES)
        re, im = np.cos(angle) / SUB, np.sin(angle) / SUB
        tables.append(np.block([[re, im], [-im, re]]))
    return jnp.asarray(np.stack(tables), jnp.bfloat16)


def taper_table():
    pos = (np.arange(SUB) - SUB // 2 + 0.5) / (SUB // 2)
    edge = 1.0 - 0.8 * pos * pos
    return jnp.asarray((edge[:, None] * edge[None, :] / NVIS).reshape(NJ, LANES), jnp.float32)


def poly(square, coefficients):
    total = jnp.full_like(square, coefficients[-1])
    for coefficient in coefficients[-2::-1]:
        total = total * square + coefficient
    return total


def cos_sin_turns(turns):
    rest = turns - jnp.round(turns)
    square = rest * rest
    sine = rest * poly(square, SIN_POLY)
    cosine = poly(square, COS_POLY)
    twice = sine + sine
    return 1.0 - twice * sine, twice * cosine


def direction_tables():
    row = lax.broadcasted_iota(jnp.int32, (2 * SUB, NVIS), 0)
    r = (row % NJ) * 4 + row // NJ
    place = jnp.where(row < SUB, r, row - SUB)
    first = (place - SUB // 2).astype(jnp.float32) * (1.0 / SUB)
    return first, -0.5 * first * first


def image_of(u, v, w, vis, first, second):
    linear = jnp.concatenate([u * first[:SUB], v * first[SUB:]], axis=0)
    cosine, sine = cos_sin_turns(linear + w * second)
    row_re, row_im = cosine[:SUB], sine[:SUB]
    col_re, col_im = cosine[SUB:], sine[SUB:]
    vis = vis.astype(jnp.float32)
    lhs = []
    for rr in range(4):
        a_re, a_im = row_re[rr * NJ:(rr + 1) * NJ], row_im[rr * NJ:(rr + 1) * NJ]
        part_re, part_im = [], []
        for e in range(NCORR):
            v_re, v_im = vis[e:e + 1], vis[NCORR + e:NCORR + e + 1]
            part_re.append(v_re * a_re - v_im * a_im)
            part_im.append(v_re * a_im + v_im * a_re)
        lhs.append(jnp.concatenate([jnp.concatenate(part_re, axis=0), jnp.concatenate(part_im, axis=0)], axis=1))
    lhs = jnp.concatenate(lhs, axis=0).astype(jnp.bfloat16)
    upper = jnp.concatenate([col_re, -col_im], axis=1)
    lower = jnp.concatenate([col_im, col_re], axis=1)
    rhs = jnp.concatenate([upper, lower, upper, lower], axis=0).astype(jnp.bfloat16)
    out = lax.dot_general(lhs, rhs, (((1,), (1,)), ((), ())), preferred_element_type=jnp.float32)
    parts = [out[rr * SUB:(rr + 1) * SUB] for rr in range(4)]
    turned = [pltpu.roll(part, SUB, 1) for part in parts]
    lane = lax.broadcasted_iota(jnp.int32, (SUB, LANES), 1)

    def join(a, b, c, d):
        return jnp.where(lane < SUB, a, jnp.where(lane < 2 * SUB, b, jnp.where(lane < 3 * SUB, c, d)))

    image_re = join(parts[0], turned[1], parts[2], turned[3])
    image_im = join(turned[0], parts[1], turned[2], parts[3])
    return image_re, image_im


def ring_plan():
    return (
        ((3, 0, 0), (1, 0, 1)),
        ((3, 0, 1), (1, 0, 0)),
        ((0, 3, 0), (0, 1, 1)),
        ((0, 3, 1), (0, 1, 0)),
        ((2, 0, 0), (2, 0, 1)),
        ((3, 3, 0), (3, 1, 1), (1, 3, 0), (1, 1, 1)),
        ((0, 2, 0), (0, 2, 1)),
        ((3, 3, 1), (3, 1, 0), (1, 3, 1), (1, 1, 0)),
        ((2, 3, 0), (2, 1, 1)),
        ((3, 2, 0), (3, 2, 1), (1, 2, 0), (1, 2, 1)),
        ((2, 3, 1), (2, 1, 0)),
        ((2, 2, 0), (2, 2, 1)),
    )


def sandwich_of(image, near, far):
    def row(array, index):
        return array[index * NJ:(index + 1) * NJ]

    mid_re, mid_im = {}, {}
    for out_row in range(2):
        for inner in range(2):
            total_re = total_im = None
            for first in range(2):
                n_re, n_im = row(near, 2 * first + out_row), row(near, 4 + 2 * first + out_row)
                v_re, v_im = row(image, 2 * first + inner), row(image, 4 + 2 * first + inner)
                re = n_re * v_re + n_im * v_im
                im = n_re * v_im - n_im * v_re
                total_re = re if total_re is None else total_re + re
                total_im = im if total_im is None else total_im + im
            mid_re[out_row, inner], mid_im[out_row, inner] = total_re, total_im
    out_re, out_im = [], []
    for out_row in range(2):
        for out_col in range(2):
            total_re = total_im = None
            for inner in range(2):
                m_re, m_im = mid_re[out_row, inner], mid_im[out_row, inner]
                f_re, f_im = row(far, 2 * inner + out_col), row(far, 4 + 2 * inner + out_col)
                re = m_re * f_re - m_im * f_im
                im = m_re * f_im + m_im * f_re
                total_re = re if total_re is None else total_re + re
                total_im = im if total_im is None else total_im + im
            out_re.append(total_re)
            out_im.append(total_im)
    return out_re, out_im


def fft8(re, im):
    def add(x, y):
        return x[0] + y[0], x[1] + y[1]

    def sub(x, y):
        return x[0] - y[0], x[1] - y[1]

    def turn(x):
        return x[1], -x[0]

    def fft4(x):
        even_add, even_sub = add(x[0], x[2]), sub(x[0], x[2])
        odd_add, odd_sub = add(x[1], x[3]), turn(sub(x[1], x[3]))
        return [add(even_add, odd_add), add(even_sub, odd_sub), sub(even_add, odd_add), sub(even_sub, odd_sub)]

    x = list(zip(re, im))
    even, odd = fft4(x[0::2]), fft4(x[1::2])
    odd = [
        odd[0],
        ((odd[1][0] + odd[1][1]) * ROOT_HALF, (odd[1][1] - odd[1][0]) * ROOT_HALF),
        turn(odd[2]),
        ((odd[3][1] - odd[3][0]) * ROOT_HALF, (-odd[3][0] - odd[3][1]) * ROOT_HALF),
    ]
    out = [add(even[k], odd[k]) for k in range(4)] + [sub(even[k], odd[k]) for k in range(4)]
    return [(-o[0], -o[1]) if k % 2 else o for k, o in enumerate(out)]


def one_hot(mask):
    return mask.astype(jnp.float32).astype(jnp.bfloat16)


def diagonal(n):
    return lax.broadcasted_iota(jnp.int32, (n, n), 0) == lax.broadcasted_iota(jnp.int32, (n, n), 1)


def as_line(column):
    n = column.shape[0]
    return jnp.sum(jnp.where(diagonal(n), jnp.broadcast_to(column, (n, n)), 0), axis=0, keepdims=True)


def slot_lines(tiles, rows, cols):
    count, slots = tiles.shape[1], NT * CAP
    shape = (count, count)
    wide = jnp.broadcast_to(tiles, shape)
    column = jnp.sum(jnp.where(diagonal(count), wide, 0), axis=1, keepdims=True)
    earlier = lax.broadcasted_iota(jnp.int32, shape, 0) < lax.broadcasted_iota(jnp.int32, shape, 1)
    rank = jnp.sum(jnp.where(earlier & (column == wide), 1, 0), axis=0, keepdims=True)
    slot = lax.broadcasted_iota(jnp.int32, (slots, count), 0)
    taken = tiles * CAP + rank == slot
    number = lax.broadcasted_iota(jnp.int32, (slots, count), 1)

    def total(values):
        return as_line(jnp.sum(jnp.where(taken, values, 0), axis=1, keepdims=True))

    return total(number), total(rows + 1) - 1, total(cols)


def grid_kernel(per_chunk, waits, per_owner, stations, own_ref, coords_ref, tiles_ref, offsets_ref, taper_ref,
                uv_far, vis_far, out_ref, shards, meta, image, x_re, x_im, y_ref, u_re, u_im, send, recv, moved, acc, order_row,
                order, places_row, places, send_sems, ring_sems, pair_sems, axis_out, axis_in, data_out, data_in, own_sem, uv_ref, vis_ref, uv_sem, vis_sem):
    corr, tile = lax.axis_index("corr"), lax.axis_index("tile")
    planes, plane = lax.axis_size("corr"), lax.axis_size("tile")
    devices = planes * plane
    core, y, z = tile & 1, (tile >> 1) & 3, tile >> 3
    count = vis_ref.shape[0]
    owned = own_ref.shape[0]
    groups_owned = shards.shape[1] - 1
    half = groups_owned // 2

    def chip(who, a, b):
        there_z = (z + who * a + (1 - who) * b) & 3
        there_y = (y + (1 - who) * a + who * b) & 3
        return (there_z * 4 + there_y) * 2 + who

    first_up, first_down = chip(core, 1, 0), chip(core, 3, 0)
    second_up, second_down = chip(core, 0, 1), chip(core, 0, 3)
    pair = (z * 4 + y) * 2 + (1 - core)
    targets = (first_up, first_down, second_up, second_down, pair)

    def along(t):
        return {"corr": (corr + t) & (planes - 1)}

    vis_load = pltpu.make_async_copy(vis_far, vis_ref, vis_sem)
    vis_load.start()
    uv_load = pltpu.make_async_copy(uv_far, uv_ref, uv_sem)
    uv_load.start()
    barrier = pltpu.get_barrier_semaphore()
    for target in targets:
        pl.semaphore_signal(barrier, inc=1, device_id={"tile": target}, device_id_type=pl.DeviceIdType.MESH)
    for t in range(1, planes):
        pl.semaphore_signal(barrier, inc=1, device_id=along(t), device_id_type=pl.DeviceIdType.MESH)

    for i in range(owned):
        screen = own_ref[i].astype(jnp.float32)
        for j in range(NJ):
            x_re[pl.ds(i * 2 * SUB + j, NJ, stride=NJ)] = screen[:, j * LANES:(j + 1) * LANES]
    for i in range(owned):
        screen = x_re[i * 2 * SUB:(i + 1) * 2 * SUB].astype(jnp.bfloat16)
        shards[tile, i * PARTS:(i + 1) * PARTS] = screen.reshape(PARTS, META, LANES)
    number_line, row_line, col_line = slot_lines(tiles_ref[...], offsets_ref[0:1], offsets_ref[1:2])
    kind = lax.broadcasted_iota(jnp.int32, (META, LANES), 0)
    lines = jnp.where(kind == 0, row_line, jnp.where(kind == 1, col_line, 0))
    shards[tile, groups_owned] = lines.astype(jnp.float32).astype(jnp.bfloat16)
    order_row[...] = number_line
    pl.semaphore_wait(barrier, len(targets) + planes - 1)

    sent = []

    def place(owner, h):
        return shards.at[owner, pl.ds(h * half, half + h)]

    def unit_index(unit):
        return (unit[0] * 4 + unit[1]) * 2 + unit[2]

    def unit_copy(owner, h, target, send_sem, sem):
        return pltpu.make_async_remote_copy(
            src_ref=place(owner, h), dst_ref=place(owner, h), send_sem=send_sem, recv_sem=sem,
            device_id={"tile": target}, device_id_type=pl.DeviceIdType.MESH,
        )

    def push(unit, target, arrives):
        sem = pair_sems.at[unit_index(unit)] if arrives is None else ring_sems.at[unit_index(arrives)]
        unit_copy(chip(core, unit[0], unit[1]), unit[2], target, send_sems.at[len(sent)], sem).start()
        sent.append(unit)

    def await_ring(unit):
        owner = chip(core, unit[0], unit[1])
        unit_copy(owner, unit[2], pair, send_sems.at[0], ring_sems.at[unit_index(unit)]).wait_recv()

    def await_pair(unit):
        owner = chip(1 - core, unit[0], unit[1])
        unit_copy(owner, unit[2], pair, send_sems.at[0], pair_sems.at[unit_index(unit)]).wait_recv()

    def forward(unit):
        a, b, h = unit
        if b == 0:
            if (a, h) == (3, 0):
                push(unit, first_up, (2, 0, 0))
            if (a, h) == (1, 1):
                push(unit, first_down, (2, 0, 1))
            up, down = (second_up, (a, 3, h)), (second_down, (a, 1, h))
            for target, arrives in (up, down) if h == 0 else (down, up):
                push(unit, target, arrives)
        elif (b, h) == (3, 0):
            push(unit, second_up, (a, 2, 0))
        elif (b, h) == (1, 1):
            push(unit, second_down, (a, 2, 1))
        push(unit, pair, None)

    push((0, 0, 0), first_up, (3, 0, 0))
    push((0, 0, 1), first_down, (1, 0, 1))
    push((0, 0, 1), first_up, (3, 0, 1))
    push((0, 0, 0), first_down, (1, 0, 0))
    push((0, 0, 0), second_up, (0, 3, 0))
    push((0, 0, 1), second_down, (0, 1, 1))
    push((0, 0, 1), second_up, (0, 3, 1))
    push((0, 0, 0), second_down, (0, 1, 0))
    for h in range(2):
        push((0, 0, h), pair, None)

    first, second = direction_tables()

    def compute(begin):
        def step(s, carry):
            u, v, w = (coords_ref[axis, pl.ds(s, 1)] for axis in range(3))
            image_re, image_im = image_of(u, v, w, vis_ref[s], first, second)
            image[s, 0:SUB] = image_re
            image[s, SUB:2 * SUB] = image_im
            return carry

        for q in range(per_chunk):
            step(begin + q, 0)

    groups = ring_plan()
    chunks = count // per_chunk

    def chunk(i, carry):
        compute(i * per_chunk)
        for group, when in zip(groups, waits):
            if when is not None:
                @pl.when(i == when)
                def _():
                    for unit in group:
                        await_ring(unit)
                        forward(unit)
        return carry

    vis_load.wait()
    lax.fori_loop(0, chunks, chunk, 0)
    uv_load.wait()
    scalars = pltpu.make_async_copy(order_row, order, own_sem)
    scalars.start()
    for group, when in zip(groups, waits):
        if when is None:
            for unit in group:
                await_ring(unit)
                forward(unit)
    for a in range(4):
        for b in range(4):
            for h in range(2):
                await_pair((a, b, h))

    shape = (2 * plane, plane * META)
    picked = lax.broadcasted_iota(jnp.int32, shape, 0)
    picked = (picked & (plane - 1)) * META + (picked >> 5) == lax.broadcasted_iota(jnp.int32, shape, 1)
    picked = one_hot(picked)
    lines = jnp.dot(picked, shards[:, groups_owned].reshape(plane * META, LANES), preferred_element_type=jnp.float32)
    meta[corr] = lines.astype(jnp.bfloat16)

    def axis_copy(t, whose):
        return pltpu.make_async_remote_copy(
            src_ref=meta.at[whose], dst_ref=meta.at[whose],
            send_sem=axis_out.at[t], recv_sem=axis_in.at[t], device_id=along(t), device_id_type=pl.DeviceIdType.MESH,
        )

    taper = taper_ref[...]

    def screen_of(station):
        screen = shards[station >> 4, pl.ds((station & (owned - 1)) * PARTS, PARTS)]
        return screen.reshape(2 * SUB, LANES).astype(jnp.float32)

    def sandwich(s, carry):
        out_re, out_im = sandwich_of(image[s], screen_of(stations[0, s]), screen_of(stations[1, s]))
        for e in range(NCORR):
            rows = pl.ds(pl.multiple_of(s * SUB + e * NJ, NJ), NJ)
            x_re[rows] = out_re[e] * taper
            x_im[rows] = out_im[e] * taper
        return carry

    lead = count // 8
    lax.fori_loop(0, lead, sandwich, 0, unroll=2)
    for t in range(1, planes):
        axis_copy(t, corr).start()
    lax.fori_loop(lead, count, sandwich, 0, unroll=2)
    points = 16

    def transform(i, carry):
        base = i * (points * NJ)
        re = [x_re[pl.ds(base + j, points, stride=NJ)] for j in range(NJ)]
        im = [x_im[pl.ds(base + j, points, stride=NJ)] for j in range(NJ)]
        rows = pl.ds(pl.multiple_of(i * points, points), points)
        for a8, (y_re, y_im) in enumerate(fft8(re, im)):
            y_ref[a8, rows, 0:LANES] = y_re.astype(jnp.bfloat16)
            y_ref[a8, rows, LANES:2 * LANES] = y_im.astype(jnp.bfloat16)
        return carry

    lax.fori_loop(0, count * NCORR // points, transform, 0)
    for a8 in range(NJ):
        out = jnp.dot(y_ref[a8], uv_ref[a8], preferred_element_type=jnp.float32)
        u_re[pl.ds(a8, count * NCORR, stride=NJ)] = out[:, 0:LANES]
        u_im[pl.ds(a8, count * NCORR, stride=NJ)] = out[:, LANES:2 * LANES]

    slots = per_owner * CAP
    scalars.wait()

    def pack(owner, carry):
        for slot in range(slots):
            s = order[0, owner * slots + slot]
            for e in range(NCORR):
                rows = pl.ds(s * SUB + e * NJ, NJ)
                both = jnp.concatenate([u_re[rows], u_im[rows]], axis=0)
                send[e * plane + owner, slot * 2 * NJ:(slot + 1) * 2 * NJ] = both.astype(jnp.bfloat16)
        return carry

    lax.fori_loop(0, plane, pack, 0)
    for t in range(1, planes):
        axis_copy(t, (corr - t) & (planes - 1)).wait()

    def there(k, sign):
        d = (k * ORDER) & (devices - 1)
        x1 = (corr + sign * (d >> 5)) & 3
        z1 = (z + sign * (d >> 3)) & 3
        y1 = (y + sign * (d >> 1)) & 3
        return x1, z1 * 8 + y1 * 2 + ((core + d) & 1)

    def data_copy(k):
        x1, t1 = there(k, 1)
        return pltpu.make_async_remote_copy(
            src_ref=send.at[x1 * plane + t1], dst_ref=recv.at[k], send_sem=data_out.at[k], recv_sem=data_in.at[k],
            device_id={"corr": x1, "tile": t1}, device_id_type=pl.DeviceIdType.MESH,
        )

    def start(k, carry):
        data_copy(k).start()
        return carry

    recv[0] = send[corr * plane + tile]
    acc[...] = jnp.zeros_like(acc)
    lax.fori_loop(1, devices, start, 0)

    line = lax.broadcasted_iota(jnp.int32, (NJ, LANES), 0)
    chosen = one_hot(lax.broadcasted_iota(jnp.int32, (NJ, LANES), 1) == tile * slots + line)
    for x in range(planes):
        part = lax.dot_general(chosen, meta[x], (((1,), (1,)), ((), ())), preferred_element_type=jnp.float32)
        places_row[x] = jnp.concatenate([part, part], axis=1).astype(jnp.int32)
    scalars = pltpu.make_async_copy(places_row, places, own_sem)
    scalars.start()
    scalars.wait()

    lane = lax.broadcasted_iota(jnp.int32, (NJ, LANES), 1)
    batch = 4
    depth = batch * CAP * SUB
    target_lane = lax.broadcasted_iota(jnp.int32, (1, depth), 1)
    target_row = lax.broadcasted_iota(jnp.int32, (TILE_SIDE, depth), 0)

    def group(g, carry):
        firsts = [jnp.zeros((1, depth), jnp.int32) for _ in range(per_owner)]
        for i in range(batch):
            k = g * batch + i

            @pl.when(k > 0)
            def _():
                data_copy(k).wait()

            x1, t1 = there(k, -1)
            for slot in range(slots):
                row0, col0 = places[x1, slot, t1], places[x1, slot, plane + t1]
                begin = jnp.where(row0 >= 0, row0, 2 * LANES)
                inside = (lane >= begin) & (lane < begin + SUB)
                block = recv[k, slot * 2 * NJ:(slot + 1) * 2 * NJ].astype(jnp.float32)
                number = i * CAP + slot % CAP
                for part in range(2):
                    data = block[part * NJ:(part + 1) * NJ]
                    rolled = []
                    for a4 in range(4):
                        shift = (row0 + (LANES - a4 * SUB)) & (LANES - 1)
                        rolled.append(jnp.where(inside, pltpu.roll(data, shift, 1), 0.0))
                    rolled = jnp.concatenate(rolled, axis=0).astype(jnp.bfloat16)
                    moved[slot // CAP, number * SUB:(number + 1) * SUB, part * LANES:(part + 1) * LANES] = rolled
                firsts[slot // CAP] = jnp.where(target_lane >= number * SUB, col0 - number * SUB, firsts[slot // CAP])
        for own_tile in range(per_owner):
            select = one_hot(target_row == firsts[own_tile] + target_lane)
            acc[own_tile] += jnp.dot(select, moved[own_tile], preferred_element_type=jnp.float32)
        return carry

    lax.fori_loop(0, devices // batch, group, 0)
    for own_tile in range(per_owner):
        for part in range(2):
            out_ref[own_tile, part] = acc[own_tile, :, part * LANES:(part + 1) * LANES].T
    for number, unit in enumerate(sent):
        unit_copy(chip(core, unit[0], unit[1]), unit[2], pair, send_sems.at[number], pair_sems.at[0]).wait_send()


WAITS = (3, 4, 5, 6, 7, 9, 11, 13, None, None, None, None)
ORDER = 37
META = 16
PARTS = 2 * SUB // META


def per_device(visibilities, coords, stations, tile_ids, offsets, screens):
    planes, plane = lax.axis_size("corr"), lax.axis_size("tile")
    devices = planes * plane
    per_owner = NT // plane
    count = visibilities.shape[0]
    points = count * NCORR
    block = (devices, per_owner * CAP * 2 * NJ, LANES)
    vmem = pl.BlockSpec(memory_space=pltpu.VMEM)
    dma = pltpu.SemaphoreType.DMA
    return pl.pallas_call(
        functools.partial(grid_kernel, 4, WAITS, per_owner),
        out_shape=jax.ShapeDtypeStruct((per_owner, 2, TILE_SIDE, TILE_SIDE), jnp.float32),
        in_specs=[pl.BlockSpec(memory_space=pltpu.SMEM)] + [vmem] * 5 + [pl.BlockSpec(memory_space=pl.ANY)] * 2,
        out_specs=vmem,
        scratch_shapes=[
            pltpu.VMEM((plane, screens.shape[0] * PARTS + 1, META, LANES), jnp.bfloat16),
            pltpu.VMEM((planes, 2 * plane, LANES), jnp.bfloat16),
            pltpu.VMEM((count, 2 * SUB, LANES), jnp.float32),
            pltpu.VMEM((points * NJ, LANES), jnp.float32),
            pltpu.VMEM((points * NJ, LANES), jnp.float32),
            pltpu.VMEM((NJ, points, 2 * LANES), jnp.bfloat16),
            pltpu.VMEM((points * NJ, LANES), jnp.float32),
            pltpu.VMEM((points * NJ, LANES), jnp.float32),
            pltpu.VMEM(block, jnp.bfloat16),
            pltpu.VMEM(block, jnp.bfloat16),
            pltpu.VMEM((per_owner, 4 * CAP * SUB, 2 * LANES), jnp.bfloat16),
            pltpu.VMEM((per_owner, TILE_SIDE, 2 * LANES), jnp.float32),
            pltpu.VMEM((1, NT * CAP), jnp.int32),
            pltpu.SMEM((1, NT * CAP), jnp.int32),
            pltpu.VMEM((planes, NJ, LANES), jnp.int32),
            pltpu.SMEM((planes, NJ, LANES), jnp.int32),
            dma((62,)),
            dma((32,)),
            dma((32,)),
            dma((planes,)),
            dma((planes,)),
            dma((devices,)),
            dma((devices,)),
            dma,
            pltpu.VMEM((NJ, 2 * LANES, 2 * LANES), jnp.bfloat16),
            pltpu.VMEM(visibilities.shape, visibilities.dtype),
            dma,
            dma,
        ],
        compiler_params=pltpu.CompilerParams(vmem_limit_bytes=VMEM_LIMIT, collective_id=0, has_side_effects=True),
        name="grid",
    )(
        stations.T, screens, coords.transpose(1, 0, 2), tile_ids.T, offsets.T, taper_table(), uv_tables(), visibilities
    )[None]


def solution(mesh):
    return jax.shard_map(
        per_device,
        mesh=mesh,
        in_specs=(
            P(("corr", "tile"), None, None),
            P(("corr", "tile"), None, None),
            P(("corr", "tile"), None),
            P(("corr", "tile"), None),
            P(("corr", "tile"), None),
            P("tile", None, None),
        ),
        out_specs=P("corr", "tile", None, None, None),
        check_vma=False,
    )
```
